256 devices in a mesh: segment: 4 (over y_lo, core), dp: 64 (over z, x, y_hi).
Axes of the slice: x: 4, y: 4 (y_hi: 2, y_lo: 2; y = y_hi * 2 + y_lo), z: 8, core: 2. Of those that a mesh axis runs over, the one named last changes fastest.
Arguments:
- images: bfloat16 [512, 256, 1024], P('dp'), may hold values from -6 to 6
- texts: bfloat16 [512, 64, 1536], P('dp'), may hold values from -6 to 6
- section_weights: bfloat16 [4, 21504, 128], P('segment'), may hold values from -0.15625 to 0.15625
- uniting_weights: bfloat16 [3584, 1024], P('dp'), may hold values from -0.125 to 0.125
- codebooks: float32 [64, 2, 256, 1024], P('dp'), may hold values from -3 to 3
- neg_bank: bfloat16 [64, 256, 1024], P('dp'), may hold values from -6 to 6
- item_cats: int32 [4, 128, 1], replicated, may hold values from 0 to 63; in each aligned block of 128 rows (0 to 127, 128 to 255, ..., all dimensions but the last counted through in order) at most 2 rows name the same one
- cat_slot: int32 [64], replicated, may hold values from 0 to 63, each once
- neg_index: int32 [4, 128, 128], replicated, may hold values from 0 to 255
Outputs:
- uniting_grad: float32 [3584, 1024], P('dp')
- codebook_grad: float32 [64, 2, 256, 1024], P('dp')
- owner_loss: float32 [64], P('dp')
The draws below stay inside these ranges and needn't reach their ends.
Inputs may be any that keep to these rules, and one draw needn't show every extreme that they name: `item_cats`: within one row of 128 no category appears more than 2 times, and in some row some category appears exactly 2 times. `cat_slot`: A permutation: every category has its own slot; slot t lies with owner t.
All inputs are finite; a program needn't handle non-finite values.
Results may differ from the reference program's by a relative error of at most 0.028.
Values may be sent and summed in bfloat16 or wider, within the bound.
A program may use at most 128 MiB of HBM per device.

```python
import math
import jax
import jax.numpy as jnp
import numpy as np
from jax import lax

D_IMG = 1024
HEAD_IMG = 64
D_TXT = 1536
HEAD_TXT = 128
EMB = 1024
PATCH = 256
TXT_LEN = 64
ITEM_DEV = 8
MERGE_DEV = 2
ITEMS = 512
CAT_DEV = 1
CATS = 64
CAP = 2
LEVELS = 2
CODES = 256
BANK = 256
NEG = 128
MERGE_IN = 2560
MERGE_ROWS = 3584
SLOT_ROWS = 21504
N_SEGMENT = 4
N_DP = 64


def draw_codebooks(key, part):
    shape_all = (CATS, LEVELS, CODES, EMB)
    values = jnp.clip(0.5 * jax.random.normal(key, shape_all, jnp.float32), -3.0, 3.0)
    return values


def set_ends(drawn, own_key, low, top_value):
    shape = drawn.shape
    spot = [jax.random.randint(jax.random.fold_in(own_key, axis), (), 0, shape[axis]) for axis in range(len(shape))]
    drawn = drawn.at[tuple(spot)].set(low)
    longest = shape.index(max(shape))
    spot[longest] = (spot[longest] + 1) % shape[longest]
    return drawn.at[tuple(spot)].set(top_value)


def steps_of(own_key, extent, split, low, top_value):
    loudness = 1.0
    for dim, blocks in split:
        steps = jax.random.uniform(jax.random.fold_in(jax.random.fold_in(own_key, 6), dim), (blocks,), jnp.float32, low / len(split), top_value / len(split))
        loudness = loudness * jnp.repeat(jnp.exp(steps), extent[dim] // blocks).reshape((-1,) + (1,) * (len(extent) - 1 - dim))
    return loudness


def deal_out(key, own, number, rows, count, top, bound, lean):
    order = jax.random.permutation(key, count)
    crowded, ordinary = shares(count, rows * top, bound, lean, True), shares(count, rows * top, bound, lean, False)
    places = jnp.arange(count)

    def named(lengths, turn):
        used = int((lengths > 0).sum())
        fixed = max(1, used // 4)
        moved = fixed + (places - fixed + turn * (used - fixed)) % max(1, count - fixed)
        return jnp.zeros((count,), jnp.int32).at[order[jnp.where(places < fixed, places, moved)]].set(jnp.asarray(lengths, jnp.int32))

    lengths = jnp.where(number % 4 == 0, named(crowded, number // 4), named(ordinary, number - number // 4 - 1))
    mixed = jax.random.permutation(jax.random.fold_in(own, 3), count)
    giver, receiver = mixed[0:count // 2 * 2:2], mixed[1:count // 2 * 2:2]
    room = jnp.minimum(lengths[giver] - 1, bound - lengths[receiver]) // 2
    room = jnp.where((giver == order[0]) | (receiver == order[0]) | (lengths[receiver] == 0), 0, jnp.maximum(room, 0))
    moved = jax.random.randint(jax.random.fold_in(own, 4), (count // 2,), 0, 1 << 20) % (room + 1)
    lengths = lengths.at[giver].add(-moved).at[receiver].add(moved)
    members = jnp.searchsorted(jnp.cumsum(lengths), jnp.arange(rows * top), side="right").astype(jnp.int32)
    table = members.reshape(top, rows).T
    table = table[jax.random.permutation(jax.random.fold_in(own, 1), rows)]
    turn = jax.random.randint(jax.random.fold_in(own, 2), (rows, 1), 0, top)
    return jnp.take_along_axis(table, (jnp.arange(top)[None, :] + turn) % top, axis=1)


def shares(number_of, total, bound, slope, full):
    weights = [(1 << 20) // math.isqrt(standing ** slope) + 1 for standing in range(1, number_of + 1)]
    largest = bound if full else min(bound, max(-(-total // number_of), total * weights[0] // sum(weights)))
    least = 1 if total - largest >= number_of - 1 else 0
    counts, surplus = [largest] + [least] * (number_of - 1), total - largest - least * (number_of - 1)
    while surplus > 0:
        free = [i for i in range(1, number_of) if counts[i] < largest] or [i for i in range(1, number_of) if counts[i] < bound]
        pool, budget = sum([weights[i] for i in free]), surplus
        for i in free:
            addition = min(bound - counts[i], max(1, budget * weights[i] // pool), surplus)
            counts[i] = counts[i] + addition
            surplus = surplus - addition
    return np.array(counts)


def gaussian(key, extent, scale, bound, pieces=(), kind=jnp.bfloat16):
    level = steps_of(key, extent, pieces, -0.22, 0.18) if pieces else 1.0
    result = jax.random.normal(key, extent, jnp.float32) * scale * level
    return jnp.minimum(jnp.maximum(result, -bound), bound).astype(kind)


def setup_inputs(seed: int = 0) -> dict:
    key_list = jax.random.split(jax.random.key(seed), 10)
    images = gaussian(key_list[0], (ITEMS, PATCH, D_IMG), 1.0, 6.0, ((0, 64),))
    texts = gaussian(key_list[1], (ITEMS, TXT_LEN, D_TXT), 1.0, 6.0, ((0, 64),))
    section_weights = gaussian(key_list[2], (N_SEGMENT, SLOT_ROWS, 128), D_TXT ** -0.5, 0.15625, ((0, 4),))
    uniting_weights = gaussian(key_list[3], (MERGE_ROWS, EMB), MERGE_IN ** -0.5, 0.125, ((0, 64),))
    codebooks = draw_codebooks(jax.random.fold_in(key_list[9], 71), 0)
    neg_bank = gaussian(key_list[5], (CATS, BANK, EMB), 1.0, 6.0, ((0, 64),))
    item_cats_keys = jax.random.split(jax.random.fold_in(key_list[6], 1), N_SEGMENT * (N_DP * MERGE_DEV) // (N_DP * MERGE_DEV))
    item_cats_turns = jax.random.permutation(jax.random.fold_in(key_list[6], 3), N_SEGMENT * (N_DP * MERGE_DEV) // (N_DP * MERGE_DEV))
    item_cats = jax.vmap(lambda own, number: deal_out(jax.random.fold_in(key_list[6], 2), own, number, N_DP * MERGE_DEV, CATS, 1, CAP, 2))(item_cats_keys, item_cats_turns).reshape((N_SEGMENT, N_DP * MERGE_DEV, 1))
    cat_slot = jax.random.permutation(key_list[7], CATS).astype(jnp.int32)
    neg_index = set_ends(jax.random.randint(key_list[8], (N_SEGMENT, N_DP * MERGE_DEV, NEG), 0, BANK), jax.random.fold_in(key_list[8], 1), 0, BANK - 1).astype(jnp.int32)
    return {"images": images, "texts": texts, "section_weights": section_weights, "uniting_weights": uniting_weights, "codebooks": codebooks, "neg_bank": neg_bank, "item_cats": item_cats, "cat_slot": cat_slot, "neg_index": neg_index}


norm_eps = 1e-06
rope_theta = 1000000.0
contrast_temp = 0.1
beta_weight = 1.0
highest = lax.Precision.HIGHEST

def operand(tensor):
    return tensor.astype(jnp.float32)

def gelu_value(inputs_f):
    return 0.5 * inputs_f * (1.0 + lax.erf(inputs_f / math.sqrt(2.0)))

def gelu_slope(inputs_f):
    return 0.5 * (1.0 + lax.erf(inputs_f / math.sqrt(2.0))) + inputs_f * jnp.exp(-0.5 * inputs_f * inputs_f) / math.sqrt(2.0 * math.pi)

def rotate_pairs(tensor, positions):
    half_dim = tensor.shape[-1] // 2
    exponents = jnp.arange(half_dim).astype(jnp.float32) * (2.0 / tensor.shape[-1])
    inverse_freq = jnp.exp(-math.log(rope_theta) * exponents)
    angles = positions[:, None] * inverse_freq[None, :]
    cosine = jnp.concatenate([jnp.cos(angles), jnp.cos(angles)], axis=-1)[:, None, :]
    sine = jnp.concatenate([jnp.sin(angles), jnp.sin(angles)], axis=-1)[:, None, :]
    rotated = jnp.concatenate([-tensor[..., half_dim:], tensor[..., :half_dim]], axis=-1)
    return tensor * cosine + rotated * sine

def softmax_rows(scores):
    scores = scores - lax.optimization_barrier(jnp.max(scores, axis=-1, keepdims=True))
    exp_scores = jnp.exp(scores)
    return (exp_scores / lax.optimization_barrier(jnp.sum(exp_scores, axis=-1, keepdims=True))).astype(jnp.bfloat16)

def image_attention(images, flat_slot):
    item_count, patch_count, model_width = images.shape
    half_width = model_width // 2
    head_count = half_width // HEAD_IMG
    qkv_size = model_width * 3 * half_width
    w_qkv = flat_slot[:qkv_size].reshape(model_width, 3 * half_width)
    w_out = flat_slot[qkv_size:qkv_size + half_width * model_width].reshape(half_width, model_width)
    float_tokens = images.astype(jnp.float32)
    centred = float_tokens - lax.optimization_barrier(jnp.mean(float_tokens, axis=-1, keepdims=True))
    variance = lax.optimization_barrier(jnp.mean(centred * centred, axis=-1, keepdims=True))
    normed = (centred * lax.rsqrt(variance + norm_eps)).astype(jnp.bfloat16)
    projections = jnp.einsum('bpd,de->bpe', operand(normed), operand(w_qkv), preferred_element_type=jnp.float32).astype(jnp.bfloat16)
    queries = projections[..., :half_width].reshape(item_count, patch_count, head_count, HEAD_IMG)
    key_rows = projections[..., half_width:2 * half_width].reshape(item_count, patch_count, head_count, HEAD_IMG)
    value_rows = projections[..., 2 * half_width:].reshape(item_count, patch_count, head_count, HEAD_IMG)
    scores = jnp.einsum('bqhc,bkhc->bhqk', operand(queries), operand(key_rows), preferred_element_type=jnp.float32) / math.sqrt(HEAD_IMG)
    probabilities = softmax_rows(scores)
    attended = jnp.einsum('bhqk,bkhc->bqhc', operand(probabilities), operand(value_rows), preferred_element_type=jnp.float32).astype(jnp.bfloat16)
    attended = attended.reshape(item_count, patch_count, half_width)
    projected = jnp.einsum('bpc,cd->bpd', operand(attended), operand(w_out), preferred_element_type=jnp.float32)
    return lax.optimization_barrier(jnp.mean(projected, axis=1))

def text_attention(texts, flat_slot):
    item_count, token_count, model_width = texts.shape
    half_width = model_width // 2
    head_count = half_width // HEAD_TXT
    inner_width = half_width + 2 * HEAD_TXT
    qkv_size = model_width * inner_width
    w_qkv = flat_slot[:qkv_size].reshape(model_width, inner_width)
    w_out = flat_slot[qkv_size:qkv_size + half_width * model_width].reshape(half_width, model_width)
    float_tokens = texts.astype(jnp.float32)
    normed = (float_tokens * lax.rsqrt(lax.optimization_barrier(jnp.mean(float_tokens * float_tokens, axis=-1, keepdims=True)) + norm_eps)).astype(jnp.bfloat16)
    projections = jnp.einsum('btd,de->bte', operand(normed), operand(w_qkv), preferred_element_type=jnp.float32)
    positions = jnp.arange(token_count).astype(jnp.float32)
    queries = rotate_pairs(projections[..., :half_width].reshape(item_count, token_count, head_count, HEAD_TXT), positions).astype(jnp.bfloat16)
    key_rows = rotate_pairs(projections[..., half_width:half_width + HEAD_TXT].reshape(item_count, token_count, 1, HEAD_TXT), positions)[:, :, 0, :].astype(jnp.bfloat16)
    value_rows = projections[..., half_width + HEAD_TXT:].astype(jnp.bfloat16)
    scores = jnp.einsum('bqhc,bkc->bhqk', operand(queries), operand(key_rows), preferred_element_type=jnp.float32) / math.sqrt(HEAD_TXT)
    causal = jnp.arange(token_count)[:, None] >= jnp.arange(token_count)[None, :]
    scores = jnp.where(causal, scores, -1e+30)
    probabilities = softmax_rows(scores)
    attended = jnp.einsum('bhqk,bkc->bqhc', operand(probabilities), operand(value_rows), preferred_element_type=jnp.float32).astype(jnp.bfloat16)
    attended = attended.reshape(item_count, token_count, half_width)
    projected = jnp.einsum('btc,cd->btd', operand(attended), operand(w_out), preferred_element_type=jnp.float32)
    return lax.optimization_barrier(jnp.mean(projected, axis=1))

def merge_forward(embedded, stacked):
    first_rows = embedded.shape[1]
    float_embed = embedded.astype(jnp.float32)
    normed = (float_embed * lax.rsqrt(lax.optimization_barrier(jnp.mean(float_embed * float_embed, axis=1, keepdims=True)) + norm_eps)).astype(jnp.bfloat16)
    hidden = jnp.dot(normed, stacked[:first_rows], preferred_element_type=jnp.float32)
    activated = gelu_value(hidden).astype(jnp.bfloat16)
    merged = jnp.dot(activated, stacked[first_rows:], preferred_element_type=jnp.float32).astype(jnp.bfloat16)
    return (normed, hidden, activated, merged)

def merge_backward(hidden, stacked, out_grad, first_rows):
    w_second = stacked[first_rows:]
    act_grad = lax.dot_general(out_grad, w_second, (((1,), (1,)), ((), ())), preferred_element_type=jnp.float32)
    return (act_grad * gelu_slope(hidden)).astype(jnp.bfloat16)

def item_loss(merged_row, book_rows, negatives):
    emb_width = merged_row.shape[0]
    quant_tau = math.sqrt(emb_width) / 2.0
    residual = merged_row * lax.rsqrt(jnp.mean(merged_row * merged_row) + norm_eps)
    quantized = jnp.zeros_like(merged_row)
    for level_index in range(book_rows.shape[0]):
        code_rows = book_rows[level_index]
        cross_terms = jnp.dot(code_rows, residual, precision=highest)
        logits = (2.0 * cross_terms - lax.optimization_barrier(jnp.sum(code_rows * code_rows, axis=1))) / quant_tau
        logits = logits - lax.stop_gradient(jnp.max(logits))
        exp_logits = jnp.exp(logits)
        chosen = jnp.dot(exp_logits / jnp.sum(exp_logits), code_rows, precision=highest)
        residual = residual - chosen
        quantized = quantized + chosen
    recon_error = jnp.mean(residual * residual)
    anchor = quantized * lax.rsqrt(jnp.mean(quantized * quantized) + norm_eps)
    candidates = jnp.concatenate([merged_row[None, :], negatives.astype(jnp.float32)], axis=0)
    cand_unit = candidates * lax.rsqrt(lax.optimization_barrier(jnp.mean(candidates * candidates, axis=1, keepdims=True)) + norm_eps)
    similarity = jnp.dot(cand_unit, anchor, precision=highest) / (emb_width * contrast_temp)
    top_score = lax.stop_gradient(jnp.max(similarity))
    contrast = top_score + jnp.log(jnp.sum(jnp.exp(similarity - top_score))) - similarity[0]
    return contrast + beta_weight * recon_error

def to_rows(tensor):
    return tensor.reshape(N_DP, N_SEGMENT, MERGE_DEV, -1).transpose(1, 0, 2, 3).reshape(N_SEGMENT * N_DP * MERGE_DEV, -1)

def from_rows(tensor):
    return tensor.reshape(N_SEGMENT, N_DP, MERGE_DEV, -1).transpose(1, 0, 2, 3).reshape(ITEMS, -1)

def reference(images, texts, section_weights, uniting_weights, codebooks, neg_bank, item_cats, cat_slot, neg_index):
    slot_table = section_weights.reshape(N_SEGMENT, -1)
    image_blocks = images.reshape(ITEMS // ITEM_DEV, ITEM_DEV, PATCH, D_IMG)
    text_blocks = texts.reshape(ITEMS // ITEM_DEV, ITEM_DEV, TXT_LEN, D_TXT)
    image_embed = lax.optimization_barrier(jnp.mean(images.astype(jnp.float32), axis=1))
    text_embed = lax.optimization_barrier(jnp.mean(texts.astype(jnp.float32), axis=1))
    for group_index in range(2):
        image_slot = slot_table[group_index]
        text_slot = slot_table[2 + group_index]
        image_embed = image_embed + lax.map(lambda item_block: image_attention(item_block, image_slot), image_blocks).reshape(ITEMS, D_IMG)
        text_embed = text_embed + lax.map(lambda item_block: text_attention(item_block, text_slot), text_blocks).reshape(ITEMS, D_TXT)
    embedded = jnp.concatenate([image_embed, text_embed], axis=1).astype(jnp.bfloat16)
    normed, hidden, activated, merged = merge_forward(embedded, uniting_weights)
    merged_rows = to_rows(merged).astype(jnp.float32)
    cats_flat = item_cats.reshape(-1).astype(jnp.int32)
    negs_flat = neg_index.reshape(-1, NEG).astype(jnp.int32)
    loss_scale = 1.0 / math.sqrt(ITEMS)

    def visit(grad_total, inputs):
        merged_row, category, negative_ids = inputs
        slot_id = cat_slot[category]
        book_rows = lax.dynamic_index_in_dim(codebooks, slot_id, 0, keepdims=False)
        bank_rows = lax.dynamic_index_in_dim(neg_bank, slot_id, 0, keepdims=False)
        negatives = jnp.take(bank_rows, negative_ids, axis=0)

        def scaled(row_value, book_value):
            return item_loss(row_value, book_value, negatives) * loss_scale
        loss_value, pullback = jax.vjp(scaled, merged_row, book_rows)
        row_grad, book_grad = pullback(jnp.ones((), jnp.float32))
        current = lax.dynamic_index_in_dim(grad_total, slot_id, 0, keepdims=False)
        grad_total = lax.dynamic_update_index_in_dim(grad_total, current + book_grad, slot_id, 0)
        return (grad_total, (row_grad, loss_value))
    book_total, (row_grads, row_losses) = lax.scan(visit, jnp.zeros(codebooks.shape, jnp.float32), (merged_rows, cats_flat, negs_flat))
    row_owner = jnp.take(cat_slot, cats_flat) // CAT_DEV
    owner_match = row_owner[None, :] == jnp.arange(N_DP)[:, None]
    owner_loss = lax.optimization_barrier(jnp.sum(jnp.where(owner_match, row_losses[None, :], 0.0), axis=1))
    out_grad = from_rows(row_grads).astype(jnp.bfloat16)
    hidden_grad = merge_backward(hidden, uniting_weights, out_grad, MERGE_IN)
    grad_first = jnp.dot(normed.T, hidden_grad, preferred_element_type=jnp.float32)
    grad_second = jnp.dot(activated.T, out_grad, preferred_element_type=jnp.float32)
    return (jnp.concatenate([grad_first, grad_second], axis=0), book_total, owner_loss)
```

```python
import math

import jax
import jax.numpy as jnp
from jax import lax
from jax.experimental import pallas as pl
from jax.experimental.pallas import tpu as pltpu
from jax.sharding import PartitionSpec as P

HEAD_IMG = 64
HEAD_TXT = 128
CAP = 2


norm_eps = 1e-06
rope_theta = 1000000.0
contrast_temp = 0.1
beta_weight = 1.0
highest = lax.Precision.HIGHEST


def gelu_value(inputs_f):
    return 0.5 * inputs_f * (1.0 + lax.erf(inputs_f / math.sqrt(2.0)))


def gelu_slope(inputs_f):
    return 0.5 * (1.0 + lax.erf(inputs_f / math.sqrt(2.0))) + inputs_f * jnp.exp(
        -0.5 * inputs_f * inputs_f
    ) / math.sqrt(2.0 * math.pi)


def rotate_pairs(tensor, positions):
    half_dim = tensor.shape[-1] // 2
    exponents = jnp.arange(half_dim).astype(jnp.float32) * (2.0 / tensor.shape[-1])
    inverse_freq = jnp.exp(-math.log(rope_theta) * exponents)
    angles = positions[:, None] * inverse_freq[None, :]
    cosine = jnp.concatenate([jnp.cos(angles), jnp.cos(angles)], axis=-1)[:, None, :]
    sine = jnp.concatenate([jnp.sin(angles), jnp.sin(angles)], axis=-1)[:, None, :]
    rotated = jnp.concatenate([-tensor[..., half_dim:], tensor[..., :half_dim]], axis=-1)
    return tensor * cosine + rotated * sine


def softmax_rows(scores):
    scores = scores - jnp.max(scores, axis=-1, keepdims=True)
    exp_scores = jnp.exp(scores)
    return (exp_scores / jnp.sum(exp_scores, axis=-1, keepdims=True)).astype(jnp.bfloat16)


def image_attention(images, flat_slot):
    item_count, patch_count, model_width = images.shape
    half_width = model_width // 2
    head_count = half_width // HEAD_IMG
    qkv_size = model_width * 3 * half_width
    w_qkv = flat_slot[:qkv_size].reshape(model_width, 3 * half_width)
    w_out = flat_slot[qkv_size : qkv_size + half_width * model_width].reshape(
        half_width, model_width
    )
    float_tokens = images.astype(jnp.float32)
    centred = float_tokens - jnp.mean(float_tokens, axis=-1, keepdims=True)
    variance = jnp.mean(centred * centred, axis=-1, keepdims=True)
    normed = (centred * lax.rsqrt(variance + norm_eps)).astype(jnp.bfloat16)
    projections = jnp.einsum(
        "bpd,de->bpe", normed, w_qkv, preferred_element_type=jnp.float32
    ).astype(jnp.bfloat16)
    queries = projections[..., :half_width].reshape(item_count, patch_count, head_count, HEAD_IMG)
    key_rows = projections[..., half_width : 2 * half_width].reshape(
        item_count, patch_count, head_count, HEAD_IMG
    )
    value_rows = projections[..., 2 * half_width :].reshape(
        item_count, patch_count, head_count, HEAD_IMG
    )
    scores = jnp.einsum(
        "bqhc,bkhc->bhqk", queries, key_rows, preferred_element_type=jnp.float32
    ) / math.sqrt(HEAD_IMG)
    probabilities = softmax_rows(scores)
    attended = jnp.einsum(
        "bhqk,bkhc->bqhc", probabilities, value_rows, preferred_element_type=jnp.float32
    ).astype(jnp.bfloat16)
    attended = attended.reshape(item_count, patch_count, half_width)
    projected = jnp.einsum("bpc,cd->bpd", attended, w_out, preferred_element_type=jnp.float32)
    return jnp.mean(projected, axis=1)


def text_attention(texts, flat_slot):
    item_count, token_count, model_width = texts.shape
    half_width = model_width // 2
    head_count = half_width // HEAD_TXT
    inner_width = half_width + 2 * HEAD_TXT
    qkv_size = model_width * inner_width
    w_qkv = flat_slot[:qkv_size].reshape(model_width, inner_width)
    w_out = flat_slot[qkv_size : qkv_size + half_width * model_width].reshape(
        half_width, model_width
    )
    float_tokens = texts.astype(jnp.float32)
    normed = (
        float_tokens
        * lax.rsqrt(jnp.mean(float_tokens * float_tokens, axis=-1, keepdims=True) + norm_eps)
    ).astype(jnp.bfloat16)
    projections = jnp.einsum("btd,de->bte", normed, w_qkv, preferred_element_type=jnp.float32)
    positions = jnp.arange(token_count).astype(jnp.float32)
    queries = rotate_pairs(
        projections[..., :half_width].reshape(item_count, token_count, head_count, HEAD_TXT),
        positions,
    ).astype(jnp.bfloat16)
    key_rows = rotate_pairs(
        projections[..., half_width : half_width + HEAD_TXT].reshape(
            item_count, token_count, 1, HEAD_TXT
        ),
        positions,
    )[:, :, 0, :].astype(jnp.bfloat16)
    value_rows = projections[..., half_width + HEAD_TXT :].astype(jnp.bfloat16)
    scores = jnp.einsum(
        "bqhc,bkc->bhqk", queries, key_rows, preferred_element_type=jnp.float32
    ) / math.sqrt(HEAD_TXT)
    causal = jnp.arange(token_count)[:, None] >= jnp.arange(token_count)[None, :]
    scores = jnp.where(causal, scores, -1e30)
    probabilities = softmax_rows(scores)
    attended = jnp.einsum(
        "bhqk,bkc->bqhc", probabilities, value_rows, preferred_element_type=jnp.float32
    ).astype(jnp.bfloat16)
    attended = attended.reshape(item_count, token_count, half_width)
    projected = jnp.einsum("btc,cd->btd", attended, w_out, preferred_element_type=jnp.float32)
    return jnp.mean(projected, axis=1)


def merge_forward(embedded, stacked):
    first_rows = embedded.shape[1]
    float_embed = embedded.astype(jnp.float32)
    normed = (
        float_embed
        * lax.rsqrt(jnp.mean(float_embed * float_embed, axis=1, keepdims=True) + norm_eps)
    ).astype(jnp.bfloat16)
    hidden = jnp.dot(normed, stacked[:first_rows], preferred_element_type=jnp.float32)
    activated = gelu_value(hidden).astype(jnp.bfloat16)
    merged = jnp.dot(activated, stacked[first_rows:], preferred_element_type=jnp.float32).astype(
        jnp.bfloat16
    )
    return (normed, hidden, activated, merged)


def merge_backward(hidden, stacked, out_grad, first_rows):
    w_second = stacked[first_rows:]
    act_grad = lax.dot_general(
        out_grad, w_second, (((1,), (1,)), ((), ())), preferred_element_type=jnp.float32
    )
    return (act_grad * gelu_slope(hidden)).astype(jnp.bfloat16)


def item_loss(merged_row, book_rows, negatives):
    emb_width = merged_row.shape[0]
    quant_tau = math.sqrt(emb_width) / 2.0
    residual = merged_row * lax.rsqrt(jnp.mean(merged_row * merged_row) + norm_eps)
    quantized = jnp.zeros_like(merged_row)
    for level_index in range(book_rows.shape[0]):
        code_rows = book_rows[level_index]
        cross_terms = jnp.dot(code_rows, residual, precision=highest)
        logits = (2.0 * cross_terms - jnp.sum(code_rows * code_rows, axis=1)) / quant_tau
        logits = logits - lax.stop_gradient(jnp.max(logits))
        exp_logits = jnp.exp(logits)
        chosen = jnp.dot(exp_logits / jnp.sum(exp_logits), code_rows, precision=highest)
        residual = residual - chosen
        quantized = quantized + chosen
    recon_error = jnp.mean(residual * residual)
    anchor = quantized * lax.rsqrt(jnp.mean(quantized * quantized) + norm_eps)
    candidates = jnp.concatenate([merged_row[None, :], negatives.astype(jnp.float32)], axis=0)
    cand_unit = candidates * lax.rsqrt(
        jnp.mean(candidates * candidates, axis=1, keepdims=True) + norm_eps
    )
    similarity = jnp.dot(cand_unit, anchor, precision=highest) / (emb_width * contrast_temp)
    top_score = lax.stop_gradient(jnp.max(similarity))
    contrast = top_score + jnp.log(jnp.sum(jnp.exp(similarity - top_score))) - similarity[0]
    return contrast + beta_weight * recon_error


def stacked_term(columns, first_grad, second_grad, in_first):
    contract = (((0,), (0,)), ((), ()))
    first_term = lax.dot_general(columns, first_grad, contract, preferred_element_type=jnp.float32)
    second_term = lax.dot_general(
        columns, second_grad, contract, preferred_element_type=jnp.float32
    )
    return jnp.where(in_first[:, None], first_term, second_term)


def gather_body(count, block_ref, out_ref, local_sem, send_sems, recv_sems):
    me = lax.axis_index("dp")
    barrier = pltpu.get_barrier_semaphore()

    def greet(step, carry):
        peer = lax.rem(me + step, count)
        pl.semaphore_signal(
            barrier, inc=1, device_id={"dp": peer}, device_id_type=pl.DeviceIdType.MESH
        )
        return carry

    lax.fori_loop(1, count, greet, 0)
    own = pltpu.make_async_copy(block_ref, out_ref.at[me], local_sem)
    own.start()
    pl.semaphore_wait(barrier, count - 1)

    def copy_to(step):
        peer = lax.rem(me + step, count)
        return pltpu.make_async_remote_copy(
            src_ref=block_ref,
            dst_ref=out_ref.at[me],
            send_sem=send_sems.at[step],
            recv_sem=recv_sems.at[step],
            device_id={"dp": peer},
            device_id_type=pl.DeviceIdType.MESH,
        )

    def send(step, carry):
        copy_to(step).start()
        return carry

    def finish(step, carry):
        copy_to(step).wait()
        return carry

    lax.fori_loop(1, count, send, 0)
    lax.fori_loop(1, count, finish, 0)
    own.wait()


def gather_dp(block, collective_id):
    count = lax.axis_size("dp")
    gathered = pl.pallas_call(
        lambda *refs: gather_body(count, *refs),
        out_shape=jax.ShapeDtypeStruct((count,) + block.shape, block.dtype),
        in_specs=[pl.BlockSpec(memory_space=pltpu.VMEM)],
        out_specs=pl.BlockSpec(memory_space=pltpu.VMEM),
        scratch_shapes=[
            pltpu.SemaphoreType.DMA,
            pltpu.SemaphoreType.DMA((count,)),
            pltpu.SemaphoreType.DMA((count,)),
        ],
        compiler_params=pltpu.CompilerParams(
            collective_id=collective_id, has_side_effects=True, vmem_limit_bytes=40 << 20
        ),
        name=f"gather_{collective_id}",
    )(block)
    return gathered.reshape((-1,) + block.shape[1:])


def per_device(
    images,
    texts,
    section_weights,
    uniting_weights,
    codebooks,
    neg_bank,
    item_cats,
    cat_slot,
    neg_index,
):
    segment_index = lax.axis_index("segment")
    segment_count = lax.axis_size("segment")
    dp_index = lax.axis_index("dp")
    dp_count = lax.axis_size("dp")
    group_index = segment_index % 2
    item_count = images.shape[0]
    flat_slot = section_weights.reshape(-1)
    residual_flag = jnp.where(group_index == 0, 1.0, 0.0).astype(jnp.float32)

    def image_branch(operands):
        image_rows, text_rows, slot_rows = operands
        pooled = image_attention(image_rows, slot_rows) + residual_flag * jnp.mean(
            image_rows.astype(jnp.float32), axis=1
        )
        return jnp.concatenate(
            [pooled, jnp.zeros((item_count, text_rows.shape[2]), jnp.float32)], axis=1
        )

    def text_branch(operands):
        image_rows, text_rows, slot_rows = operands
        pooled = text_attention(text_rows, slot_rows) + residual_flag * jnp.mean(
            text_rows.astype(jnp.float32), axis=1
        )
        return jnp.concatenate(
            [jnp.zeros((item_count, image_rows.shape[2]), jnp.float32), pooled], axis=1
        )

    packed = lax.cond(segment_index < 2, image_branch, text_branch, (images, texts, flat_slot))
    embedded = lax.psum_scatter(packed, "segment", scatter_dimension=0, tiled=True).astype(
        jnp.bfloat16
    )
    stacked = gather_dp(uniting_weights, 1)
    first_rows = embedded.shape[1]
    cat_per_dev = codebooks.shape[0]
    slot_count = cat_per_dev * CAP
    row_total = item_cats.shape[1]
    cats_all = item_cats.reshape(-1)
    entry_count = cats_all.shape[0]
    entry_ids = jnp.arange(entry_count)
    category_match = cats_all[:, None] == jnp.arange(cat_slot.shape[0])[None, :]
    entry_slots = jnp.sum(jnp.where(category_match, cat_slot[None, :], 0), axis=1)
    entry_owner = entry_slots // cat_per_dev
    entry_local = entry_slots % cat_per_dev
    entry_row = entry_ids // row_total
    earlier = entry_ids[None, :] < entry_ids[:, None]
    same_cat = (cats_all[:, None] == cats_all[None, :]) & (entry_row[:, None] == entry_row[None, :])
    entry_rank = jnp.sum(jnp.where(earlier & same_cat, 1, 0), axis=1)
    entry_place = entry_local * CAP + entry_rank
    entry_position = entry_row * slot_count + entry_place
    owned = entry_owner == dp_index
    all_slots = segment_count * slot_count
    slot_match_all = owned[None, :] & (entry_position[None, :] == jnp.arange(all_slots)[:, None])
    view_match = lax.dynamic_slice(
        slot_match_all,
        (segment_index * slot_count, segment_index * row_total),
        (slot_count, row_total),
    )
    view_base = segment_index * row_total
    view_slots = view_match.shape[0]
    selection = view_match.astype(jnp.bfloat16)
    valid = jnp.sum(view_match.astype(jnp.float32), axis=1)
    slot_item = jnp.sum(
        jnp.where(view_match, jnp.arange(view_match.shape[1])[None, :] + view_base, 0), axis=1
    )
    slot_negs = jnp.take(neg_index.reshape(entry_count, -1), slot_item, axis=0)
    slot_local = jnp.arange(view_slots) % slot_count // CAP
    bank_rows = neg_bank.reshape(-1, neg_bank.shape[2])
    negatives = jnp.take(bank_rows, slot_local[:, None] * neg_bank.shape[1] + slot_negs, axis=0)
    loss_scale = 1.0 / math.sqrt(dp_count * item_count)

    def owner_objective(merged_float, books):
        per_row = jax.vmap(item_loss)(merged_float, books[slot_local], negatives)
        return jnp.sum(per_row * valid) * loss_scale

    gathered = jnp.dot(
        selection,
        gather_dp(embedded, 2),
        preferred_element_type=jnp.float32,
    )
    gathered = gathered.astype(jnp.bfloat16)
    normed_all, hidden_all, activated_all, merged_all = merge_forward(gathered, stacked)
    loss_local, pullback = jax.vjp(owner_objective, merged_all.astype(jnp.float32), codebooks)
    grad_all, book_grad = pullback(jnp.ones((), jnp.float32))
    out_grad = grad_all.astype(jnp.bfloat16)
    hidden_grad = merge_backward(hidden_all, stacked, out_grad, first_rows)
    joined = jnp.concatenate([normed_all, activated_all], axis=1)
    book_total, loss_owner = lax.psum((book_grad, loss_local), "segment")
    shard_rows = uniting_weights.shape[0]
    shard_start = dp_index * shard_rows
    shard_first = shard_start + jnp.arange(shard_rows) < first_rows
    joined_piece = gather_dp(joined, 3)
    first_piece = gather_dp(hidden_grad, 4)
    second_piece = gather_dp(out_grad, 5)
    columns = lax.dynamic_slice_in_dim(joined_piece, shard_start, shard_rows, 1)
    segment_grad = stacked_term(columns, first_piece, second_piece, shard_first)
    uniting_grad = lax.psum(segment_grad, "segment")
    return (uniting_grad, book_total, loss_owner.reshape(1))


def solution(mesh):
    placed = (
        P("dp", None, None),
        P("dp", None, None),
        P("segment", None, None),
        P("dp", None),
        P("dp", None, None, None),
        P("dp", None, None),
        P(),
        P(),
        P(),
    )
    return jax.shard_map(
        per_device,
        mesh=mesh,
        in_specs=placed,
        out_specs=(P("dp", None), P("dp", None, None, None), P("dp")),
        check_vma=False,
    )
```

```python
import math

import jax
import jax.numpy as jnp
import numpy as np
from jax import lax
from jax.experimental import pallas as pl
from jax.experimental.pallas import tpu as pltpu
from jax.sharding import PartitionSpec as P

MESH = pl.DeviceIdType.MESH
BF = jnp.bfloat16
F32 = jnp.float32
HEAD_IMG = 64
HEAD_TXT = 128
CAP = 2
SEG = 4
NZ = 8
NQ = 8
NDP = 64

norm_eps = 1e-06
rope_theta = 1000000.0
contrast_temp = 0.1
NT = (((1,), (1,)), ((), ()))
TN = (((0,), (0,)), ((), ()))
NN = (((1,), (0,)), ((), ()))


def dot(a, b, dims=NN):
    return lax.dot_general(a, b, dims, preferred_element_type=F32)


def iota(shape, axis):
    return lax.broadcasted_iota(jnp.int32, shape, axis)


def split(a):
    high = a.astype(BF)
    return high, (a - high.astype(F32)).astype(BF)


def dot3(a, pair, dims):
    rows = a.shape[0]
    high, low = split(a)
    both = dot(jnp.concatenate([high, low], axis=0), pair[0], dims)
    return both[:rows] + both[rows:] + dot(high, pair[1], dims)


def unit_scale(a):
    return lax.rsqrt(jnp.mean(a * a, axis=1, keepdims=True) + norm_eps)


def relayout(slot, stage, first, rows, blocks, dest):
    group = 64

    def step(index, carry):
        base = pl.multiple_of(first + index * (group * blocks), 64)
        stage[pl.ds(0, group * blocks), :] = slot[pl.ds(base, group * blocks), :].astype(F32)
        at = pl.multiple_of(index * group, group)
        for block in range(blocks):
            dest[pl.ds(at, group), block * 128 : (block + 1) * 128] = stage[
                pl.ds(block, group, stride=blocks), :
            ].astype(BF)
        return carry

    lax.fori_loop(0, rows // group, step, 0)


def attend(scores):
    size = scores.shape[0]
    total = None
    for start in range(0, size, 64):
        part = scores[start : start + 64]
        top = jnp.max(part, axis=1, keepdims=True)
        probs = jnp.exp(part - top)
        probs = probs * (1.0 / jnp.sum(probs, axis=1, keepdims=True))
        folded = jnp.sum(probs.reshape(8, 8, size), axis=0)
        total = folded if total is None else total + folded
    return jnp.sum(total, axis=0, keepdims=True)


def image_part(flag, img, slot, stage, wi, wio, xn, qk, ysum, means, pool_row, img_sems, images):
    relayout(slot, stage, 0, 1024, 12, wi)
    relayout(slot, stage, 12288, 512, 8, wio)
    lane = iota((1, 128), 1)
    masks = (lane < 64, lane >= 64)

    def item(index, carry):
        pltpu.make_async_copy(images.at[index], img.at[index], img_sems.at[index]).wait()
        total = None
        for start in range(0, 256, 32):
            rows = img[index, start : start + 32, :].astype(F32)
            part = jnp.sum(rows.reshape(4, 8, 1024), axis=0)
            total = part if total is None else total + part
            centred = rows - jnp.mean(rows, axis=1, keepdims=True)
            xn[start : start + 32, 0:1024] = (centred * unit_scale(centred)).astype(BF)
        means[pl.ds(index, 1), 0:1024] = jnp.sum(total, axis=0, keepdims=True) * (1.0 / 256.0)
        normed = xn[:, 0:1024]
        qk[...] = dot(normed, wi[:, 0:1024]).astype(BF)
        sums = []
        for pair in range(4):
            query = qk[:, pair * 128 : (pair + 1) * 128] * BF(1.0 / math.sqrt(HEAD_IMG))
            keys = qk[:, 512 + pair * 128 : 512 + (pair + 1) * 128]
            for mask in masks:
                sums.append(attend(dot(jnp.where(mask, query, BF(0.0)), keys, NT)))
        weights = (jnp.concatenate(sums, axis=0) * (1.0 / 256.0)).astype(BF)
        ysum[pl.ds(pl.multiple_of(index * 8, 8), 8), :] = dot(weights, normed)
        return carry

    lax.fori_loop(0, 8, item, 0)
    values = dot(ysum[...].astype(BF), wi[:, 1024:1536])
    head = iota((64, 512), 0) % 8
    own = jnp.where(iota((64, 512), 1) // HEAD_IMG == head, values, 0.0)
    attended = jnp.sum(own.reshape(8, 8, 512), axis=1).astype(BF)
    pool_row[:, 0:1024] = dot(attended, wio[...]) + flag * means[:, 0:1024]
    pool_row[:, 1024:1536] = jnp.zeros((8, 512), F32)


def text_part(flag, txt, slot, stage, wt, wto, xn, cos_ref, sin_ref, attended, means, pool_row):
    relayout(slot, stage, 0, 1536, 8, wt)
    relayout(slot, stage, 12288, 768, 12, wto)
    attended[...] = jnp.zeros((8, 768), F32)
    means[...] = jnp.zeros((8, 1536), F32)
    row, column = iota((256, 256), 0), iota((256, 256), 1)
    causal = (row // 64 == column // 64) & (column <= row)
    cosine, sine = cos_ref[...], sin_ref[...]

    def rotate(tensor):
        return (tensor * cosine + pltpu.roll(tensor, 64, 1) * sine).astype(BF)

    def half(index, carry):
        base = pl.multiple_of(index * 256, 256)
        for start in range(0, 256, 32):
            rows = txt[pl.ds(base + start, 32), :].astype(F32)
            xn[start : start + 32, :] = (rows * unit_scale(rows)).astype(BF)
        member = jnp.where(
            iota((8, 256), 0) == index * 4 + iota((8, 256), 1) // 64, 1.0 / 64.0, 0.0
        )
        means[...] += dot(member.astype(BF), txt[pl.ds(base, 256), :])
        projected = dot(xn[...], wt[...])
        keys = rotate(projected[:, 768:896])
        values = projected[:, 896:1024].astype(BF)
        for head in range(6):
            query = rotate(projected[:, head * 128 : (head + 1) * 128])
            scores = dot(query, keys, NT) * (1.0 / math.sqrt(HEAD_TXT))
            weights = attend(jnp.where(causal, scores, -1e30))
            attended[:, head * 128 : (head + 1) * 128] += dot(
                (weights * member).astype(BF), values
            )
        return carry

    lax.fori_loop(0, 2, half, 0)
    pool_row[...] = dot(attended[...].astype(BF), wto[...]) + flag * means[...]


def encode_body(
    images, texts, section, unit, cos_ref, sin_ref,
    pool, wcol,
    slot, stage, wi, wio, wt, wto, img, txt, xn, qk, ysum, means, attended, mine,
    slot_sem, img_sems, txt_sem, own_sem, w_send, w_recv, s_send, s_recv,
):
    seg, me = lax.axis_index("segment"), lax.axis_index("dp")
    block = seg ^ (2 * (me % 2))
    is_image = seg < 2
    flag = jnp.where(seg % 2 == 0, 1.0, 0.0)
    barrier = pltpu.get_barrier_semaphore()

    def peer_of(step):
        peer = lax.rem(me + step, NDP)
        return {"segment": block ^ (2 * (peer % 2)), "dp": peer}

    def greet(step, carry):
        pl.semaphore_signal(barrier, inc=1, device_id=peer_of(step), device_id_type=MESH)
        return carry

    lax.fori_loop(1, NDP, greet, 0)
    for step in range(1, SEG):
        pl.semaphore_signal(
            barrier, inc=1, device_id={"segment": lax.rem(seg + step, SEG)}, device_id_type=MESH
        )
    slot_copy = pltpu.make_async_copy(section, slot, slot_sem)
    slot_copy.start()
    txt_copy = pltpu.make_async_copy(texts, txt, txt_sem)

    @pl.when(is_image)
    def _():
        def fetch(index, carry):
            pltpu.make_async_copy(images.at[index], img.at[index], img_sems.at[index]).start()
            return carry

        lax.fori_loop(0, 8, fetch, 0)

    @pl.when(jnp.logical_not(is_image))
    def _():
        txt_copy.start()

    columns = pl.ds(pl.multiple_of(block * 256, 256), 256)
    own = pltpu.make_async_copy(unit.at[:, columns], wcol.at[me], own_sem)
    own.start()
    pl.semaphore_wait(barrier, NDP - 1 + SEG - 1)

    def w_copy(step):
        return pltpu.make_async_remote_copy(
            src_ref=unit.at[:, columns],
            dst_ref=wcol.at[me],
            send_sem=w_send.at[step],
            recv_sem=w_recv.at[step],
            device_id=peer_of(step),
            device_id_type=MESH,
        )

    def w_start(step, carry):
        w_copy(step).start()
        return carry

    lax.fori_loop(1, NDP, w_start, 0)
    slot_copy.wait()

    @pl.when(is_image)
    def _():
        image_part(
            flag, img, slot, stage, wi, wio, xn, qk, ysum, means, mine, img_sems, images
        )

    @pl.when(jnp.logical_not(is_image))
    def _():
        txt_copy.wait()
        text_part(flag, txt, slot, stage, wt, wto, xn, cos_ref, sin_ref, attended, means, mine)

    def pool_copy(step):
        return pltpu.make_async_remote_copy(
            src_ref=mine,
            dst_ref=pool.at[seg],
            send_sem=s_send.at[step],
            recv_sem=s_recv.at[step],
            device_id={"segment": lax.rem(seg + step, SEG)},
            device_id_type=MESH,
        )

    for step in range(1, SEG):
        pool_copy(step).start()
    pool[seg] = mine[...]

    def w_finish(step, carry):
        w_copy(step).wait()
        return carry

    lax.fori_loop(1, NDP, w_finish, 0)
    own.wait()
    for step in range(1, SEG):
        pool_copy(step).wait()


def encode(images, texts, section, unit):
    half = HEAD_TXT // 2
    exponents = np.arange(half, dtype=np.float32) * np.float32(2.0 / HEAD_TXT)
    inverse = np.exp(np.float32(-math.log(rope_theta)) * exponents).astype(np.float32)
    angles = np.arange(64, dtype=np.float32)[:, None] * inverse[None, :]
    cosine = np.tile(np.cos(angles), (4, 2)).astype(np.float32)
    sine = np.tile(np.concatenate([-np.sin(angles), np.sin(angles)], axis=1), (4, 1))
    anywhere = pl.BlockSpec(memory_space=pl.ANY)
    vmem = pl.BlockSpec(memory_space=pltpu.VMEM)
    dma = pltpu.SemaphoreType.DMA
    return pl.pallas_call(
        encode_body,
        out_shape=(
            jax.ShapeDtypeStruct((SEG, 8, 1536), F32),
            jax.ShapeDtypeStruct((NDP, 56, 256), BF),
        ),
        in_specs=[anywhere, anywhere, anywhere, vmem, vmem, vmem],
        out_specs=(vmem, anywhere),
        scratch_shapes=[
            pltpu.VMEM((21504, 128), BF),
            pltpu.VMEM((768, 128), F32),
            pltpu.VMEM((1024, 1536), BF),
            pltpu.VMEM((512, 1024), BF),
            pltpu.VMEM((1536, 1024), BF),
            pltpu.VMEM((768, 1536), BF),
            pltpu.VMEM((8, 256, 1024), BF),
            pltpu.VMEM((512, 1536), BF),
            pltpu.VMEM((256, 1536), BF),
            pltpu.VMEM((256, 1024), BF),
            pltpu.VMEM((64, 1024), F32),
            pltpu.VMEM((8, 1536), F32),
            pltpu.VMEM((8, 768), F32),
            pltpu.VMEM((8, 1536), F32),
            dma, dma((8,)), dma, dma, dma((NDP,)), dma((NDP,)), dma((SEG,)), dma((SEG,)),
        ],
        compiler_params=pltpu.CompilerParams(
            collective_id=0, has_side_effects=True, vmem_limit_bytes=60 << 20
        ),
        name="encode",
    )(
        images,
        texts.reshape(512, 1536),
        section.reshape(21504, 128),
        unit,
        jnp.asarray(cosine, F32),
        jnp.asarray(sine, F32),
    )


def softmax(logits):
    exps = jnp.exp(logits - jnp.max(logits, axis=1, keepdims=True))
    return exps / jnp.sum(exps, axis=1, keepdims=True)


def row_total(a):
    return jnp.sum(a, axis=1, keepdims=True)


def slot_ids(cats, rows, keys, cats_col, slot_col):
    named = iota((NDP, 512), 0) == cats
    owner = jnp.sum(jnp.where(named, slot_col, 0.0), axis=0, keepdims=True)
    rank = jnp.zeros((8, 512), F32)
    for start in range(0, 512, 64):
        entry = iota((64, 1), 0) + start
        earlier = (
            (cats_col[start : start + 64] == cats)
            & (entry // 128 == rows)
            & (entry % 128 < keys)
        )
        rank = rank + jnp.sum(jnp.where(earlier, 1.0, 0.0).reshape(8, 8, 512), axis=0)
    rank = jnp.sum(rank, axis=0, keepdims=True)
    return owner.astype(jnp.int32), rows * CAP + rank.astype(jnp.int32)


def quantize(m, valid, counts, codes, code_norms, bank, bank_scale, loss_scale):
    width = m.shape[1]
    slope = 4.0 / math.sqrt(width)
    sharp = 1.0 / (width * contrast_temp)
    merged_scale = unit_scale(m)
    start = m * merged_scale
    residual = start
    trail = []
    for level in range(2):
        logits = dot3(residual, codes[level], NT) * slope - code_norms[level] * (0.5 * slope)
        probs = softmax(logits)
        chosen = dot3(probs, codes[level], NN)
        trail.append((residual, probs, chosen))
        residual = residual - chosen
    quantized = trail[0][2] + trail[1][2]
    anchor_scale = unit_scale(quantized)
    anchor = quantized * anchor_scale
    high, low = split(anchor)
    both = dot(jnp.concatenate([high, low], axis=0), bank, NT)
    used = counts > 0.0
    sims = jnp.where(used, (both[:8] + both[8:]) * bank_scale * sharp, -1e30)
    first = row_total(anchor * start) * sharp
    top = jnp.maximum(first, jnp.max(sims, axis=1, keepdims=True))
    first_exp = jnp.exp(first - top)
    bank_exp = counts * jnp.exp(sims - top)
    total = first_exp + row_total(bank_exp)
    recon = jnp.mean(residual * residual, axis=1, keepdims=True)
    loss = (top + jnp.log(total) - first + recon) * valid * loss_scale

    scale = valid * loss_scale
    first_grad = scale * (first_exp / total - 1.0) * sharp
    high, low = split(scale * bank_exp / total * bank_scale * sharp)
    both = dot(jnp.concatenate([high, low], axis=0), bank, NN)
    anchor_grad = first_grad * start + both[:8] + both[8:]
    start_grad = first_grad * anchor
    quant_grad = anchor_scale * (
        anchor_grad - anchor * jnp.mean(anchor * anchor_grad, axis=1, keepdims=True)
    )
    res_grad = residual * (scale * (2.0 / width))
    factors = [None, None]
    for level in (1, 0):
        before, probs, chosen = trail[level]
        chosen_grad = quant_grad - res_grad
        prob_grad = dot3(chosen_grad, codes[level], NT)
        logit_grad = probs * (prob_grad - row_total(probs * prob_grad)) * slope
        res_grad = res_grad + dot3(logit_grad, codes[level], NN)
        factors[level] = (probs, logit_grad, chosen_grad, before)
    start_grad = start_grad + res_grad
    merged_grad = merged_scale * (
        start_grad - start * jnp.mean(start * start_grad, axis=1, keepdims=True)
    )
    return loss, merged_grad, factors


def book_gradient(level, factor, books, bgrad):
    probs, logit_grad, chosen_grad, before = factor
    left_high, left_low = split(jnp.concatenate([probs, logit_grad], axis=0))
    right_high, right_low = split(jnp.concatenate([chosen_grad, before], axis=0))
    left = jnp.concatenate([left_high, left_high, left_low], axis=0)
    right = jnp.concatenate([right_high, right_low, right_high], axis=0)
    sums = dot(
        jnp.concatenate([left_high[8:], left_low[8:]], axis=0), jnp.ones((16, 256), BF), TN
    )
    for start in range(0, 1024, 256):
        at = slice(start, start + 256)
        bgrad[level, :, at] = dot(left, right[:, at], TN) - books[level, :, at] * sums


def train_body(
    pool, wcol, books, bank, cats_row, cats_col, cats_item, slot_col, neg,
    ugrad, bgrad, loss_ref,
    wv, act_buf, za, xo, xi, ms, ogs, rs_out, rs_in, gz, got, got2, jt, jz, jx, second, chigh, clow,
    w_sem, a_send, a_recv, m_send, m_recv, r_send, r_recv, u_send, u_recv,
    z1_send, z1_recv, q1_send, q1_recv, z2_send, z2_recv, q2_send, q2_recv, q3_send, q3_recv,
    zj_send, zj_recv, qj_send, qj_recv,
):
    seg, me = lax.axis_index("segment"), lax.axis_index("dp")
    z, q = me // NQ, me % NQ
    flip = 2 * (me % 2)
    block = seg ^ flip
    barrier = pltpu.get_barrier_semaphore()

    def seg_peer(step):
        return {"segment": lax.rem(seg + step, SEG)}

    def z_of(step):
        return lax.rem(z + step, NZ)

    def q_of(step):
        return lax.rem(q + step, NQ)

    def z_peer(step):
        return {"segment": seg, "dp": z_of(step) * NQ + q}

    def q_peer(step):
        return {"segment": block ^ (2 * (q_of(step) % 2)), "dp": z * NQ + q_of(step)}

    def remote(src, dst, send, recv, step, peer):
        return pltpu.make_async_remote_copy(
            src_ref=src,
            dst_ref=dst,
            send_sem=send.at[step],
            recv_sem=recv.at[step],
            device_id=peer,
            device_id_type=MESH,
        )

    def start_all(copies):
        for copy in copies:
            copy.start()

    def wait_all(copies):
        for copy in copies:
            copy.wait()

    for count, peer in ((SEG, seg_peer), (NZ, z_peer), (NQ, q_peer)):
        for step in range(1, count):
            pl.semaphore_signal(barrier, inc=1, device_id=peer(step), device_id_type=MESH)
    w_copy = pltpu.make_async_copy(wcol, wv, w_sem)
    w_copy.start()

    embedded = jnp.concatenate(
        [pool[0, :, 0:1024] + pool[1, :, 0:1024], pool[2] + pool[3]], axis=1
    )
    embedded = embedded.astype(BF).astype(F32)
    normed = (embedded * unit_scale(embedded)).astype(BF)
    w_copy.wait()
    hidden = dot(normed, wv[0:2560, :])
    bell = 0.5 * (1.0 + lax.erf(hidden * (1.0 / math.sqrt(2.0))))
    act_buf[block] = (hidden * bell).astype(BF)
    bell = bell + hidden * jnp.exp(-0.5 * hidden * hidden) * (1.0 / math.sqrt(2.0 * math.pi))
    pl.semaphore_wait(barrier, SEG + NZ + NQ - 3)
    a_copies = [
        remote(act_buf.at[block], act_buf.at[block], a_send, a_recv, step, seg_peer(step))
        for step in range(1, SEG)
    ]
    start_all(a_copies)

    lanes = iota((1, 512), 1)
    owner_e, place_e = slot_ids(
        cats_row[...], lanes // 128, lanes % 128, cats_col, slot_col[...]
    )
    item_dp = (lanes // 8 % 8) * 8 + lanes // 64
    item_row, item_key = lanes % 8 // 2, item_dp * 2 + lanes % 2
    owner_i, place_i = slot_ids(cats_item[...], item_row, item_key, cats_col, slot_col[...])
    select = iota((64, 512), 0) + z * 64 == owner_i * 8 + place_i
    fold = iota((512, 64), 0) == iota((512, 64), 1) + q * 64
    select = dot(
        jnp.where(select, 1.0, 0.0).astype(BF), jnp.where(fold, 1.0, 0.0).astype(BF)
    ).astype(BF)

    wait_all(a_copies)
    act = jnp.concatenate([act_buf[index] for index in range(SEG)], axis=1)
    merged = dot(act, wv[2560:3584, :])
    za[z] = jnp.concatenate([merged, bell], axis=0).astype(BF)
    z1_copies = [
        remote(za.at[z], za.at[z], z1_send, z1_recv, step, z_peer(step)) for step in range(1, NZ)
    ]
    start_all(z1_copies)

    joined = jnp.concatenate(
        [normed.astype(F32), act.astype(F32), jnp.zeros((8, 128), F32)], axis=1
    )
    for index in range(NDP):
        jt[index] = joined[:, index * 56 : index * 56 + 128].astype(BF)
    zj_copies = [
        remote(
            jt.at[pl.ds(pl.multiple_of(z_of(step) * NQ, NQ), NQ)],
            jz.at[z], zj_send, zj_recv, step, z_peer(step),
        )
        for step in range(1, NZ)
    ]
    start_all(zj_copies)
    jz[z] = jt[pl.ds(pl.multiple_of(z * NQ, NQ), NQ)]

    wait_all(z1_copies)
    arrived = za[...].astype(F32)
    xo[:, 0:8, :] = dot(select, arrived[:, 0:8].reshape(64, 256).astype(BF)).reshape(8, 8, 256).astype(BF)
    xo[:, 8:16, :] = dot(select, arrived[:, 8:16].reshape(64, 256).astype(BF)).reshape(8, 8, 256).astype(BF)
    q1_copies = [
        remote(xo.at[q_of(step)], xi.at[q], q1_send, q1_recv, step, q_peer(step))
        for step in range(1, NQ)
    ]
    start_all(q1_copies)
    xi[q] = xo[q]

    own = jnp.where(owner_e * 8 + place_e == iota((8, 512), 0) + me * 8, 1.0, 0.0)
    valid = row_total(own)
    picked = dot(neg[...].astype(F32).astype(BF), own.astype(BF), (((0,), (1,)), ((), ())))
    bins = iota((128, 256), 1).astype(F32)
    counts = jnp.concatenate(
        [
            jnp.sum(jnp.where(picked[:, k : k + 1] == bins, 1.0, 0.0), axis=0, keepdims=True)
            for k in range(8)
        ],
        axis=0,
    )
    ones = jnp.ones((8, 1024), BF)
    code_norms = []
    for level in range(2):
        for start in range(0, 256, 64):
            rows = slice(start, start + 64)
            high, low = split(books[level, rows, :])
            chigh[level, rows, :] = high
            clow[level, rows, :] = low
        high, low = split(books[level] * books[level])
        code_norms.append((dot(ones, high, NT) + dot(ones, low, NT))[0:1])
    wide = bank[...].astype(F32)
    high, low = split(wide * wide)
    bank_scale = lax.rsqrt(
        (dot(ones, high, NT) + dot(ones, low, NT))[0:1] * (1.0 / 1024.0) + norm_eps
    )

    wait_all(q1_copies)
    total = jnp.sum(xi[...].astype(F32), axis=0)
    bell = total[8:16]
    ms[block] = total[0:8].astype(BF)
    m_copies = [
        remote(ms.at[block], ms.at[block], m_send, m_recv, step, seg_peer(step))
        for step in range(1, SEG)
    ]
    start_all(m_copies)
    wait_all(zj_copies)
    qj_copies = [
        remote(jz.at[:, q_of(step)], jx.at[q], qj_send, qj_recv, step, q_peer(step))
        for step in range(1, NQ)
    ]
    start_all(qj_copies)
    jx[q] = jz[:, q]
    wait_all(m_copies)

    rows = jnp.concatenate([ms[index].astype(F32) for index in range(SEG)], axis=1)
    codes = [(chigh[level], clow[level]) for level in range(2)]
    loss, merged_grad, factors = quantize(
        rows, valid, counts, codes, code_norms, bank[...], bank_scale, 1.0 / math.sqrt(512.0)
    )
    loss_ref[...] = jnp.broadcast_to(jnp.sum(loss, axis=0, keepdims=True), (8, 128))
    out_grad = merged_grad.astype(BF)
    for index in range(SEG):
        ogs[index] = out_grad[:, index * 256 : (index + 1) * 256]
    partial = dot(ogs[block], wv[2560:3584, :], NT)
    for index in range(SEG):
        rs_out[index] = partial[:, index * 256 : (index + 1) * 256]
    r_copies = [
        remote(
            rs_out.at[lax.rem(seg + step, SEG) ^ flip], rs_in.at[block],
            r_send, r_recv, step, seg_peer(step),
        )
        for step in range(1, SEG)
    ]
    start_all(r_copies)
    rs_in[block] = rs_out[block]
    gz[1, z] = ogs[block]
    book_gradient(0, factors[0], books, bgrad)
    wait_all(r_copies)
    gz[0, z] = (jnp.sum(rs_in[...], axis=0) * bell).astype(BF)
    z2_copies = [
        remote(gz.at[:, z], gz.at[:, z], z2_send, z2_recv, step, z_peer(step))
        for step in range(1, NZ)
    ]
    start_all(z2_copies)
    book_gradient(1, factors[1], books, bgrad)
    wait_all(z2_copies)

    q2_copies = [
        remote(
            gz.at[(z * NQ + q_of(step)) // 46], got.at[q], q2_send, q2_recv, step, q_peer(step)
        )
        for step in range(1, NQ)
    ]
    start_all(q2_copies)
    q3_copies = [
        remote(gz.at[1], got2.at[q], q3_send, q3_recv, step, q_peer(step))
        for step in range(1, NQ)
    ]
    for step in range(1, NQ):

        @pl.when(z * NQ + q_of(step) == 45)
        def _(step=step):
            q3_copies[step - 1].start()

    got[q] = gz[me // 46]
    wait_all(qj_copies)
    columns = jx[...].astype(F32).reshape(512, 128).astype(BF)
    slots = iota((512, 512), 0) == (owner_i % 8) * 64 + (owner_i // 8) * 8 + place_i
    columns = dot(jnp.where(slots, 1.0, 0.0).astype(BF), columns).astype(BF)
    wait_all(q2_copies)
    grads = got[...].astype(F32).reshape(512, 256).astype(BF)
    second[...] = dot(columns, grads, TN)[0:56]

    @pl.when(me == 45)
    def _():
        got2[q] = gz[1]
        for copy in q3_copies:
            copy.wait_recv()
        others = dot(columns, got2[...].astype(F32).reshape(512, 256).astype(BF), TN)[0:56]
        second[...] = jnp.where(iota((56, 256), 0) < 2560 - 45 * 56, second[...], others)

    for step in range(1, NQ):

        @pl.when(z * NQ + q_of(step) == 45)
        def _(step=step):
            q3_copies[step - 1].wait_send()

    at = pl.ds(pl.multiple_of(block * 256, 256), 256)
    ugrad[:, at] = second[...]
    u_copies = [
        remote(ugrad.at[:, at], ugrad.at[:, at], u_send, u_recv, step, seg_peer(step))
        for step in range(1, SEG)
    ]
    start_all(u_copies)
    wait_all(u_copies)


def train(pool, wcol, books, bank, item_cats, cat_slot, neg_index):
    anywhere = pl.BlockSpec(memory_space=pl.ANY)
    vmem = pl.BlockSpec(memory_space=pltpu.VMEM)
    dma = pltpu.SemaphoreType.DMA
    cats = item_cats.reshape(512)
    by_item = item_cats.reshape(SEG, NZ, NQ, 2).transpose(2, 1, 0, 3)
    return pl.pallas_call(
        train_body,
        out_shape=(
            jax.ShapeDtypeStruct((56, 1024), F32),
            jax.ShapeDtypeStruct((2, 256, 1024), F32),
            jax.ShapeDtypeStruct((8, 128), F32),
        ),
        in_specs=[vmem, anywhere] + [vmem] * 7,
        out_specs=(vmem, vmem, vmem),
        scratch_shapes=[
            pltpu.VMEM((3584, 256), BF),
            pltpu.VMEM((SEG, 8, 256), BF),
            pltpu.VMEM((NZ, 16, 256), BF),
            pltpu.VMEM((NQ, 16, 256), BF),
            pltpu.VMEM((NQ, 16, 256), BF),
            pltpu.VMEM((SEG, 8, 256), BF),
            pltpu.VMEM((SEG, 8, 256), BF),
            pltpu.VMEM((SEG, 8, 256), F32),
            pltpu.VMEM((SEG, 8, 256), F32),
            pltpu.VMEM((2, NZ, 8, 256), BF),
            pltpu.VMEM((NQ, NZ, 8, 256), BF),
            pltpu.VMEM((NQ, NZ, 8, 256), BF),
            pltpu.VMEM((NDP, 8, 128), BF),
            pltpu.VMEM((NZ, NQ, 8, 128), BF),
            pltpu.VMEM((NQ, NZ, 8, 128), BF),
            pltpu.VMEM((56, 256), F32),
            pltpu.VMEM((2, 256, 1024), BF),
            pltpu.VMEM((2, 256, 1024), BF),
            dma,
        ]
        + [dma((SEG,))] * 8
        + [dma((8,))] * 14,
        compiler_params=pltpu.CompilerParams(
            collective_id=1, has_side_effects=True, vmem_limit_bytes=60 << 20
        ),
        name="train",
    )(
        pool,
        wcol.reshape(3584, 256),
        books.reshape(2, 256, 1024),
        bank.reshape(256, 1024),
        cats.reshape(1, 512),
        cats.reshape(512, 1),
        by_item.reshape(1, 512),
        cat_slot.astype(F32).reshape(NDP, 1),
        neg_index.reshape(512, 128),
    )


def per_device(
    images, texts, section_weights, uniting_weights, codebooks, neg_bank, item_cats, cat_slot, neg_index
):
    pool, wcol = encode(images, texts, section_weights, uniting_weights)
    ugrad, bgrad, loss = train(pool, wcol, codebooks, neg_bank, item_cats, cat_slot, neg_index)
    return ugrad, bgrad.reshape(codebooks.shape), loss[0:1, 0].reshape(1)


def solution(mesh):
    placed = (
        P("dp", None, None),
        P("dp", None, None),
        P("segment", None, None),
        P("dp", None),
        P("dp", None, None, None),
        P("dp", None, None),
        P(),
        P(),
        P(),
    )
    return jax.shard_map(
        per_device,
        mesh=mesh,
        in_specs=placed,
        out_specs=(P("dp", None), P("dp", None, None, None), P("dp")),
        check_vma=False,
    )
```

```python
import math

import jax
import jax.numpy as jnp
import numpy as np
from jax import lax
from jax.experimental import pallas as pl
from jax.experimental.pallas import tpu as pltpu
from jax.sharding import PartitionSpec as P

MESH = pl.DeviceIdType.MESH
BF = jnp.bfloat16
F32 = jnp.float32
HEAD_IMG = 64
HEAD_TXT = 128
CAP = 2
SEG = 4
NZ = 8
NQ = 8
NDP = 64
IMAGE_LEGS = (2, 5)

norm_eps = 1e-06
rope_theta = 1000000.0
contrast_temp = 0.1
NT = (((1,), (1,)), ((), ()))
TN = (((0,), (0,)), ((), ()))
NN = (((1,), (0,)), ((), ()))


def dot(a, b, dims=NN):
    return lax.dot_general(a, b, dims, preferred_element_type=F32)


def iota(shape, axis):
    return lax.broadcasted_iota(jnp.int32, shape, axis)


def split(a):
    high = a.astype(BF)
    return high, (a - high.astype(F32)).astype(BF)


def dot3(a, pair, dims):
    rows = a.shape[0]
    high, low = split(a)
    both = dot(jnp.concatenate([high, low], axis=0), pair[0], dims)
    return both[:rows] + both[rows:] + dot(high, pair[1], dims)


def unit_scale(a):
    return lax.rsqrt(jnp.mean(a * a, axis=1, keepdims=True) + norm_eps)


def relayout(slot, stage, first, rows, blocks, dest):
    group = 64

    def step(index, carry):
        base = pl.multiple_of(first + index * (group * blocks), 64)
        stage[pl.ds(0, group * blocks), :] = slot[pl.ds(base, group * blocks), :].astype(F32)
        at = pl.multiple_of(index * group, group)
        for block in range(blocks):
            dest[pl.ds(at, group), block * 128 : (block + 1) * 128] = stage[
                pl.ds(block, group, stride=blocks), :
            ].astype(BF)
        return carry

    lax.fori_loop(0, rows // group, step, 0)


def attend(scores):
    size = scores.shape[0]
    total = None
    for start in range(0, size, 64):
        part = scores[start : start + 64]
        top = jnp.max(part, axis=1, keepdims=True)
        probs = jnp.exp(part - top)
        probs = probs * (1.0 / jnp.sum(probs, axis=1, keepdims=True))
        folded = jnp.sum(probs.reshape(8, 8, size), axis=0)
        total = folded if total is None else total + folded
    return jnp.sum(total, axis=0, keepdims=True)


def image_part(flag, img, slot, stage, wi, wio, xn, qk, ysum, means, pool_row, img_sems, images, legs):
    relayout(slot, stage, 0, 1024, 12, wi)
    relayout(slot, stage, 12288, 512, 8, wio)
    lane = iota((1, 128), 1)
    masks = (lane < 64, lane >= 64)

    def item(index, carry):
        for at, leg in zip(IMAGE_LEGS, legs):
            pl.when(index == at)(leg)
        pltpu.make_async_copy(images.at[index], img.at[index], img_sems.at[index]).wait()
        total = None
        for start in range(0, 256, 32):
            rows = img[index, start : start + 32, :].astype(F32)
            part = jnp.sum(rows.reshape(4, 8, 1024), axis=0)
            total = part if total is None else total + part
            centred = rows - jnp.mean(rows, axis=1, keepdims=True)
            xn[start : start + 32, 0:1024] = (centred * unit_scale(centred)).astype(BF)
        means[pl.ds(index, 1), 0:1024] = jnp.sum(total, axis=0, keepdims=True) * (1.0 / 256.0)
        normed = xn[:, 0:1024]
        qk[...] = dot(normed, wi[:, 0:1024]).astype(BF)
        sums = []
        for pair in range(4):
            query = qk[:, pair * 128 : (pair + 1) * 128] * BF(1.0 / math.sqrt(HEAD_IMG))
            keys = qk[:, 512 + pair * 128 : 512 + (pair + 1) * 128]
            for mask in masks:
                sums.append(attend(dot(jnp.where(mask, query, BF(0.0)), keys, NT)))
        weights = (jnp.concatenate(sums, axis=0) * (1.0 / 256.0)).astype(BF)
        ysum[pl.ds(pl.multiple_of(index * 8, 8), 8), :] = dot(weights, normed)
        return carry

    lax.fori_loop(0, 8, item, 0)
    values = dot(ysum[...].astype(BF), wi[:, 1024:1536])
    head = iota((64, 512), 0) % 8
    own = jnp.where(iota((64, 512), 1) // HEAD_IMG == head, values, 0.0)
    attended = jnp.sum(own.reshape(8, 8, 512), axis=1).astype(BF)
    pool_row[:, 0:1024] = dot(attended, wio[...]) + flag * means[:, 0:1024]
    pool_row[:, 1024:1536] = jnp.zeros((8, 512), F32)


def text_part(flag, txt, slot, stage, wt, wto, xn, cos_ref, sin_ref, attended, means, pool_row, legs):
    relayout(slot, stage, 0, 1536, 8, wt)
    relayout(slot, stage, 12288, 768, 12, wto)
    attended[...] = jnp.zeros((8, 768), F32)
    means[...] = jnp.zeros((8, 1536), F32)
    row, column = iota((256, 256), 0), iota((256, 256), 1)
    causal = (row // 64 == column // 64) & (column <= row)
    cosine, sine = cos_ref[...], sin_ref[...]

    def rotate(tensor):
        return (tensor * cosine + pltpu.roll(tensor, 64, 1) * sine).astype(BF)

    def half(index, carry):
        for at, leg in enumerate(legs):
            pl.when(index == at)(leg)
        base = pl.multiple_of(index * 256, 256)
        for start in range(0, 256, 32):
            rows = txt[pl.ds(base + start, 32), :].astype(F32)
            xn[start : start + 32, :] = (rows * unit_scale(rows)).astype(BF)
        member = jnp.where(
            iota((8, 256), 0) == index * 4 + iota((8, 256), 1) // 64, 1.0 / 64.0, 0.0
        )
        means[...] += dot(member.astype(BF), txt[pl.ds(base, 256), :])
        projected = dot(xn[...], wt[...])
        keys = rotate(projected[:, 768:896])
        values = projected[:, 896:1024].astype(BF)
        for head in range(6):
            query = rotate(projected[:, head * 128 : (head + 1) * 128])
            scores = dot(query, keys, NT) * (1.0 / math.sqrt(HEAD_TXT))
            weights = attend(jnp.where(causal, scores, -1e30))
            attended[:, head * 128 : (head + 1) * 128] += dot(
                (weights * member).astype(BF), values
            )
        return carry

    lax.fori_loop(0, 2, half, 0)
    pool_row[...] = dot(attended[...].astype(BF), wto[...]) + flag * means[...]


def encode_body(
    images, texts, section, unit, cos_ref, sin_ref,
    pool, wcol, wv,
    slot, stage, wi, wio, wt, wto, img, txt, xn, qk, ysum, means, attended, mine,
    slot_sem, img_sems, txt_sem, own_sem, w_sem, s_send, s_recv,
    a_send, a_recv, b_send, b_recv, c_send, c_recv, d_send, d_recv, e_send, e_recv,
    early,
):
    seg, me = lax.axis_index("segment"), lax.axis_index("dp")
    block = seg ^ (2 * (me % 2))
    is_image = seg < 2
    flag = jnp.where(seg % 2 == 0, 1.0, 0.0)
    a_sems, b_sems, c_sems = (a_send, a_recv), (b_send, b_recv), (c_send, c_recv)
    d_sems, e_sems = (d_send, d_recv), (e_send, e_recv)
    barrier = pltpu.get_barrier_semaphore()
    z, q = me // NQ, me % NQ

    def z_at(step):
        return lax.rem(z + step + NZ, NZ)

    def q_at(step):
        return lax.rem(q + step, NQ)

    def z_peer(step):
        return {"segment": seg, "dp": z_at(step) * NQ + q}

    def q_peer(step):
        return {"segment": block ^ (2 * (q_at(step) % 2)), "dp": z * NQ + q_at(step)}

    def seg_peer(step):
        return {"segment": lax.rem(seg + step, SEG)}

    for count, peer in ((SEG, seg_peer), (NZ, z_peer), (NQ, q_peer)):
        for step in range(1, count):
            pl.semaphore_signal(barrier, inc=1, device_id=peer(step), device_id_type=MESH)
    slot_copy = pltpu.make_async_copy(section, slot, slot_sem)
    slot_copy.start()
    txt_copy = pltpu.make_async_copy(texts, txt, txt_sem)
    for copy in early:
        copy.start()

    @pl.when(is_image)
    def _():
        def fetch(index, carry):
            pltpu.make_async_copy(images.at[index], img.at[index], img_sems.at[index]).start()
            return carry

        lax.fori_loop(0, 8, fetch, 0)

    @pl.when(jnp.logical_not(is_image))
    def _():
        txt_copy.start()

    columns = pl.ds(pl.multiple_of(block * 256, 256), 256)
    own = pltpu.make_async_copy(unit.at[:, columns], wcol.at[z, pl.ds(pl.multiple_of(q * 56, 8), 56)], own_sem)
    own.start()

    left, right = slice(0, 128), slice(128, 256)
    left_in = unit.at[:, pl.ds(pl.multiple_of(block * 256, 128), 128)]
    right_in = unit.at[:, pl.ds(pl.multiple_of(block * 256 + 128, 128), 128)]

    def remote(src, dst, pair, index, peer):
        return pltpu.make_async_remote_copy(
            src_ref=src,
            dst_ref=dst,
            send_sem=pair[0].at[index],
            recv_sem=pair[1].at[index],
            device_id=peer,
            device_id_type=MESH,
        )

    def same(ref, pair, index, peer):
        return remote(ref, ref, pair, index, peer)

    first = [
        remote(left_in, wcol.at[z, pl.ds(pl.multiple_of(q * 56, 8), 56), left], a_sems, step, q_peer(step)) for step in range(1, NQ)
    ] + [
        remote(right_in, wcol.at[z, pl.ds(pl.multiple_of(q * 56, 8), 56), right], b_sems, step, z_peer(step))
        for step in range(1, NZ)
    ]
    middle = [
        same(wcol.at[z, :, left], c_sems, index, z_peer(shift))
        for index, shift in enumerate((1, -1, 2, -2))
    ] + [same(wcol.at[:, pl.ds(pl.multiple_of(q * 56, 8), 56), right], d_sems, step, q_peer(step)) for step in range(1, NQ)]
    last = [
        same(wcol.at[z_at(-2), :, left], e_sems, 0, z_peer(1)),
        same(wcol.at[z_at(2), :, left], e_sems, 1, z_peer(-1)),
        same(wcol.at[z_at(-2), 0:224, left], e_sems, 2, z_peer(2)),
        same(wcol.at[z_at(2), 224:448, left], e_sems, 3, z_peer(-2)),
    ]

    def second_leg():
        own.wait()
        for copy in first:
            copy.wait()
        for copy in middle:
            copy.start()

    def third_leg():
        for copy in middle[2:4]:
            copy.wait()
        for copy in last:
            copy.start()

    pl.semaphore_wait(barrier, SEG + NZ + NQ - 3)
    for copy in first:
        copy.start()
    slot_copy.wait()

    @pl.when(is_image)
    def _():
        image_part(
            flag, img, slot, stage, wi, wio, xn, qk, ysum, means, mine, img_sems, images,
            (second_leg, third_leg),
        )

    @pl.when(jnp.logical_not(is_image))
    def _():
        txt_copy.wait()
        text_part(flag, txt, slot, stage, wt, wto, xn, cos_ref, sin_ref, attended, means, mine, (second_leg, third_leg))

    def pool_copy(step):
        return pltpu.make_async_remote_copy(
            src_ref=mine,
            dst_ref=pool.at[seg],
            send_sem=s_send.at[step],
            recv_sem=s_recv.at[step],
            device_id=seg_peer(step),
            device_id_type=MESH,
        )

    for step in range(1, SEG):
        pool_copy(step).start()
    pool[seg] = mine[...]

    for copy in middle[:2] + middle[4:] + last:
        copy.wait()
    w_copies = [
        pltpu.make_async_copy(wcol.at[index], wv.at[pl.ds(index * 448, 448)], w_sem.at[index])
        for index in range(NZ)
    ]
    for copy in w_copies:
        copy.start()
    for step in range(1, SEG):
        pool_copy(step).wait()
    return w_copies


def softmax(logits):
    exps = jnp.exp(logits - jnp.max(logits, axis=1, keepdims=True))
    return exps / jnp.sum(exps, axis=1, keepdims=True)


def row_total(a):
    return jnp.sum(a, axis=1, keepdims=True)


def slot_tables(cats_ref, slot_ref):
    cats = jnp.concatenate([cats_ref[...].astype(F32), jnp.zeros((4, 128), F32)], axis=0)
    slots = jnp.broadcast_to(slot_ref[...].astype(F32), (8, NDP)).astype(BF)
    square = iota((128, 128), 0), iota((128, 128), 1)
    turned = dot(jnp.where(square[0] == square[1], 1.0, 0.0).astype(BF), cats.astype(BF), NT)
    lanes = iota((1, 512), 1)
    keys = ((lanes // 8 % 8) * 8 + lanes // 64) * 2 + lanes % 2
    by_row, by_item = [], jnp.zeros((8, 512), F32)
    for row in range(SEG):
        named = cats[row : row + 1]
        owner = dot(
            slots, jnp.where(iota((NDP, 128), 0).astype(F32) == named, 1.0, 0.0).astype(BF)
        )
        earlier = (turned[:, row : row + 1] == named) & (square[0] < square[1])
        rank = jnp.sum(jnp.where(earlier, 1.0, 0.0), axis=0, keepdims=True)
        place = row * CAP + rank
        both = jnp.where(iota((8, 128), 0) == 0, owner, place)
        by_row.append((owner[0:1] * 8.0 + place).astype(jnp.int32))
        moved = (iota((128, 512), 0) == keys) & (lanes % 8 // 2 == row)
        by_item = by_item + dot(both.astype(BF), jnp.where(moved, 1.0, 0.0).astype(BF))
    by_item = by_item.astype(jnp.int32)
    return jnp.concatenate(by_row, axis=1), by_item[0:1], by_item[1:2]


def quantize(m, valid, counts, codes, code_norms, bank, bank_scale, loss_scale):
    width = m.shape[1]
    slope = 4.0 / math.sqrt(width)
    sharp = 1.0 / (width * contrast_temp)
    merged_scale = unit_scale(m)
    start = m * merged_scale
    residual = start
    trail = []
    for level in range(2):
        logits = dot3(residual, codes[level], NT) * slope - code_norms[level] * (0.5 * slope)
        probs = softmax(logits)
        chosen = dot3(probs, codes[level], NN)
        trail.append((residual, probs, chosen))
        residual = residual - chosen
    quantized = trail[0][2] + trail[1][2]
    anchor_scale = unit_scale(quantized)
    anchor = quantized * anchor_scale
    high, low = split(anchor)
    both = dot(jnp.concatenate([high, low], axis=0), bank, NT)
    used = counts > 0.0
    sims = jnp.where(used, (both[:8] + both[8:]) * bank_scale * sharp, -1e30)
    first = row_total(anchor * start) * sharp
    top = jnp.maximum(first, jnp.max(sims, axis=1, keepdims=True))
    first_exp = jnp.exp(first - top)
    bank_exp = counts * jnp.exp(sims - top)
    total = first_exp + row_total(bank_exp)
    recon = jnp.mean(residual * residual, axis=1, keepdims=True)
    loss = (top + jnp.log(total) - first + recon) * valid * loss_scale

    scale = valid * loss_scale
    first_grad = scale * (first_exp / total - 1.0) * sharp
    high, low = split(scale * bank_exp / total * bank_scale * sharp)
    both = dot(jnp.concatenate([high, low], axis=0), bank, NN)
    anchor_grad = first_grad * start + both[:8] + both[8:]
    start_grad = first_grad * anchor
    quant_grad = anchor_scale * (
        anchor_grad - anchor * jnp.mean(anchor * anchor_grad, axis=1, keepdims=True)
    )
    res_grad = residual * (scale * (2.0 / width))
    factors = [None, None]
    for level in (1, 0):
        before, probs, chosen = trail[level]
        chosen_grad = quant_grad - res_grad
        prob_grad = dot3(chosen_grad, codes[level], NT)
        logit_grad = probs * (prob_grad - row_total(probs * prob_grad)) * slope
        res_grad = res_grad + dot3(logit_grad, codes[level], NN)
        factors[level] = (probs, logit_grad, chosen_grad, before)
    start_grad = start_grad + res_grad
    merged_grad = merged_scale * (
        start_grad - start * jnp.mean(start * start_grad, axis=1, keepdims=True)
    )
    return loss, merged_grad, factors


def book_factors(factor):
    probs, logit_grad, chosen_grad, before = factor
    left_high, left_low = split(jnp.concatenate([probs, logit_grad], axis=0))
    right_high, right_low = split(jnp.concatenate([chosen_grad, before], axis=0))
    left = jnp.concatenate([left_high, left_high, left_low], axis=0)
    right = jnp.concatenate([right_high, right_low, right_high], axis=0)
    return left, right


def finish_body(left, right, books, blocks, loss_in, ugrad, bgrad, loss):
    rows = iota((48, 256), 0)
    mask = jnp.where(((rows >= 8) & (rows < 16)) | (rows >= 40), 1.0, 0.0).astype(BF)
    sums = dot(left[0], mask, TN)
    for start in range(0, 1024, 256):
        at = slice(start, start + 256)
        bgrad[0, :, at] = dot(left[0], right[0, :, at], TN) - books[0, :, at] * sums
    for index in range(SEG):
        ugrad[:, index * 256 : (index + 1) * 256] = blocks[index].astype(F32)
    loss[0] = jnp.max(loss_in[...])


def finish(left, right, books, blocks, loss):
    smem = pl.BlockSpec(memory_space=pltpu.SMEM)
    return pl.pallas_call(
        finish_body,
        grid=(2, 2),
        out_shape=(
            jax.ShapeDtypeStruct((56, 1024), F32),
            jax.ShapeDtypeStruct((2, 256, 1024), F32),
            jax.ShapeDtypeStruct((1,), F32),
        ),
        in_specs=[
            pl.BlockSpec((1, 48, 128), lambda i, j: (i, 0, j)),
            pl.BlockSpec((1, 48, 1024), lambda i, j: (i, 0, 0)),
            pl.BlockSpec((1, 128, 1024), lambda i, j: (i, j, 0)),
            pl.BlockSpec((SEG, 56, 256), lambda i, j: (0, 0, 0)),
            pl.BlockSpec((8, 128), lambda i, j: (0, 0)),
        ],
        out_specs=(
            pl.BlockSpec((56, 1024), lambda i, j: (0, 0)),
            pl.BlockSpec((1, 128, 1024), lambda i, j: (i, j, 0)),
            smem,
        ),
        name="finish",
    )(left, right, books, blocks, loss)


def train_body(
    pool, w_copies, books, bank, cats, slots, neg, book_copies, bank_copy, neg_copy,
    blocks, left_ref, right_ref, loss_ref,
    wv, act_buf, za, xo, xi, ms, ogs, r2, gz, got, got2, jt, jz, jx, second, chigh, clow,
    own_sem, a_send, a_recv, m_send, m_recv, r_send, r_recv, u_send, u_recv,
    z1_send, z1_recv, q1_send, q1_recv, z2_send, z2_recv, q2_send, q2_recv, q3_send, q3_recv,
    zj_send, zj_recv, qj_send, qj_recv,
):
    seg, me = lax.axis_index("segment"), lax.axis_index("dp")
    z, q = me // NQ, me % NQ
    flip = 2 * (me % 2)
    block = seg ^ flip

    def seg_peer(step):
        return {"segment": lax.rem(seg + step, SEG)}

    def z_of(step):
        return lax.rem(z + step, NZ)

    def q_of(step):
        return lax.rem(q + step, NQ)

    def z_peer(step):
        return {"segment": seg, "dp": z_of(step) * NQ + q}

    def q_peer(step):
        return {"segment": block ^ (2 * (q_of(step) % 2)), "dp": z * NQ + q_of(step)}

    def remote(src, dst, send, recv, step, peer):
        return pltpu.make_async_remote_copy(
            src_ref=src,
            dst_ref=dst,
            send_sem=send.at[step],
            recv_sem=recv.at[step],
            device_id=peer,
            device_id_type=MESH,
        )

    def start_all(copies):
        for copy in copies:
            copy.start()

    def wait_all(copies):
        for copy in copies:
            copy.wait()

    embedded = jnp.concatenate(
        [pool[0, :, 0:1024] + pool[1, :, 0:1024], pool[2] + pool[3]], axis=1
    )
    embedded = embedded.astype(BF).astype(F32)
    normed = (embedded * unit_scale(embedded)).astype(BF)
    for copy in w_copies:
        copy.wait()
    hidden = dot(normed, wv[0:2560, :])
    bell = 0.5 * (1.0 + lax.erf(hidden * (1.0 / math.sqrt(2.0))))
    act_buf[block] = (hidden * bell).astype(BF)
    bell = bell + hidden * jnp.exp(-0.5 * hidden * hidden) * (1.0 / math.sqrt(2.0 * math.pi))
    a_copies = [
        remote(act_buf.at[block], act_buf.at[block], a_send, a_recv, step, seg_peer(step))
        for step in range(1, SEG)
    ]
    start_all(a_copies)

    by_entry, owner_i, place_i = slot_tables(cats, slots)
    select = iota((64, 512), 0) + z * 64 == owner_i * 8 + place_i
    fold = iota((512, 64), 0) == iota((512, 64), 1) + q * 64
    select = dot(
        jnp.where(select, 1.0, 0.0).astype(BF), jnp.where(fold, 1.0, 0.0).astype(BF)
    ).astype(BF)

    wait_all(a_copies)
    act = jnp.concatenate([act_buf[index] for index in range(SEG)], axis=1)
    merged = dot(act, wv[2560:3584, :])
    za[z] = jnp.concatenate([merged, bell], axis=0).astype(BF)
    z1_copies = [
        remote(za.at[z], za.at[z], z1_send, z1_recv, step, z_peer(step)) for step in range(1, NZ)
    ]
    start_all(z1_copies)

    def w2_rows(index):
        return wv.at[pl.ds(pl.multiple_of(2560 + index * 256, 256), 256)]

    r_copies = [
        remote(
            w2_rows(lax.rem(seg + step, SEG) ^ flip), r2.at[block],
            r_send, r_recv, step, seg_peer(step),
        )
        for step in range(1, SEG)
    ]
    start_all(r_copies)
    own_rows = pltpu.make_async_copy(w2_rows(block), r2.at[block], own_sem)
    own_rows.start()

    joined = jnp.concatenate(
        [normed.astype(F32), act.astype(F32), jnp.zeros((8, 128), F32)], axis=1
    )
    for index in range(NDP):
        jt[index] = joined[:, index * 56 : index * 56 + 128].astype(BF)
    zj_copies = [
        remote(
            jt.at[pl.ds(pl.multiple_of(z_of(step) * NQ, NQ), NQ)],
            jz.at[z], zj_send, zj_recv, step, z_peer(step),
        )
        for step in range(1, NZ)
    ]
    start_all(zj_copies)
    jz[z] = jt[pl.ds(pl.multiple_of(z * NQ, NQ), NQ)]

    wait_all(z1_copies)
    arrived = za[...].astype(F32)
    xo[:, 0:8, :] = dot(select, arrived[:, 0:8].reshape(64, 256).astype(BF)).reshape(8, 8, 256).astype(BF)
    xo[:, 8:16, :] = dot(select, arrived[:, 8:16].reshape(64, 256).astype(BF)).reshape(8, 8, 256).astype(BF)
    q1_copies = [
        remote(xo.at[q_of(step)], xi.at[q], q1_send, q1_recv, step, q_peer(step))
        for step in range(1, NQ)
    ]
    start_all(q1_copies)
    xi[q] = xo[q]

    neg_copy.wait()
    bank_copy.wait()
    for copy in book_copies:
        copy.wait()
    own = jnp.where(by_entry == iota((8, 512), 0) + me * 8, 1.0, 0.0)
    valid = row_total(own)
    picked = dot(neg[...].astype(F32).astype(BF), own.astype(BF), (((0,), (1,)), ((), ())))
    bins = iota((128, 256), 1).astype(F32)
    counts = jnp.concatenate(
        [
            jnp.sum(jnp.where(picked[:, k : k + 1] == bins, 1.0, 0.0), axis=0, keepdims=True)
            for k in range(8)
        ],
        axis=0,
    )
    ones = jnp.ones((8, 1024), BF)
    code_norms = []
    for level in range(2):
        for start in range(0, 256, 64):
            rows = slice(start, start + 64)
            high, low = split(books[level, rows, :])
            chigh[level, rows, :] = high
            clow[level, rows, :] = low
        high, low = split(books[level] * books[level])
        code_norms.append((dot(ones, high, NT) + dot(ones, low, NT))[0:1])
    wide = bank[...].astype(F32)
    high, low = split(wide * wide)
    bank_scale = lax.rsqrt(
        (dot(ones, high, NT) + dot(ones, low, NT))[0:1] * (1.0 / 1024.0) + norm_eps
    )

    wait_all(q1_copies)
    total = jnp.sum(xi[...].astype(F32), axis=0)
    bell = total[8:16]
    ms[block] = total[0:8].astype(BF)
    m_copies = [
        remote(ms.at[block], ms.at[block], m_send, m_recv, step, seg_peer(step))
        for step in range(1, SEG)
    ]
    start_all(m_copies)
    wait_all(zj_copies)
    qj_copies = [
        remote(jz.at[:, q_of(step)], jx.at[q], qj_send, qj_recv, step, q_peer(step))
        for step in range(1, NQ)
    ]
    start_all(qj_copies)
    jx[q] = jz[:, q]
    wait_all(m_copies)

    rows = jnp.concatenate([ms[index].astype(F32) for index in range(SEG)], axis=1)
    codes = [(chigh[level], clow[level]) for level in range(2)]
    loss, merged_grad, factors = quantize(
        rows, valid, counts, codes, code_norms, bank[...], bank_scale, 1.0 / math.sqrt(512.0)
    )
    loss_ref[...] = jnp.broadcast_to(jnp.sum(loss, axis=0, keepdims=True), (8, 128))
    out_grad = merged_grad.astype(BF)
    for index in range(SEG):
        ogs[index] = out_grad[:, index * 256 : (index + 1) * 256]
    own_rows.wait()
    wait_all(r_copies)
    act_grad = dot(ogs[0], r2[0], NT)
    for index in range(1, SEG):
        act_grad = act_grad + dot(ogs[index], r2[index], NT)
    gz[1, z] = ogs[block]
    gz[0, z] = (act_grad * bell).astype(BF)
    z2_copies = [
        remote(gz.at[:, z], gz.at[:, z], z2_send, z2_recv, step, z_peer(step))
        for step in range(1, NZ)
    ]
    start_all(z2_copies)
    for level in range(2):
        left_ref[level], right_ref[level] = book_factors(factors[level])
    wait_all(z2_copies)

    q2_copies = [
        remote(
            gz.at[(z * NQ + q_of(step)) // 46], got.at[q], q2_send, q2_recv, step, q_peer(step)
        )
        for step in range(1, NQ)
    ]
    start_all(q2_copies)
    q3_copies = [
        remote(gz.at[1], got2.at[q], q3_send, q3_recv, step, q_peer(step))
        for step in range(1, NQ)
    ]
    for step in range(1, NQ):

        @pl.when(z * NQ + q_of(step) == 45)
        def _(step=step):
            q3_copies[step - 1].start()

    got[q] = gz[me // 46]
    wait_all(qj_copies)
    columns = jx[...].astype(F32).reshape(512, 128).astype(BF)
    slots = iota((512, 512), 0) == (owner_i % 8) * 64 + (owner_i // 8) * 8 + place_i
    columns = dot(jnp.where(slots, 1.0, 0.0).astype(BF), columns).astype(BF)
    wait_all(q2_copies)
    grads = got[...].astype(F32).reshape(512, 256).astype(BF)
    second[...] = dot(columns, grads, TN)[0:56]

    @pl.when(me == 45)
    def _():
        got2[q] = gz[1]
        for copy in q3_copies:
            copy.wait_recv()
        others = dot(columns, got2[...].astype(F32).reshape(512, 256).astype(BF), TN)[0:56]
        second[...] = jnp.where(iota((56, 256), 0) < 2560 - 45 * 56, second[...], others)

    for step in range(1, NQ):

        @pl.when(z * NQ + q_of(step) == 45)
        def _(step=step):
            q3_copies[step - 1].wait_send()

    blocks[block] = second[...].astype(BF)
    u_copies = [
        remote(blocks.at[block], blocks.at[block], u_send, u_recv, step, seg_peer(step))
        for step in range(1, SEG)
    ]
    start_all(u_copies)
    wait_all(u_copies)


ENCODE_VMEM = (
    ((SEG, 8, 1536), F32),
    ((3584, 256), BF),
    ((21504, 128), BF),
    ((768, 128), F32),
    ((1024, 1536), BF),
    ((512, 1024), BF),
    ((1536, 1024), BF),
    ((768, 1536), BF),
    ((8, 256, 1024), BF),
    ((512, 1536), BF),
    ((256, 1536), BF),
    ((256, 1024), BF),
    ((64, 1024), F32),
    ((8, 1536), F32),
    ((8, 768), F32),
    ((8, 1536), F32),
)
ENCODE_SEMS = (0, 8, 0, 0, 8, SEG, SEG, 8, 8, 8, 8, 4, 4, 8, 8, 4, 4)
TRAIN_VMEM = (
    ((SEG, 8, 256), BF),
    ((NZ, 16, 256), BF),
    ((NQ, 16, 256), BF),
    ((NQ, 16, 256), BF),
    ((SEG, 8, 256), BF),
    ((SEG, 8, 256), BF),
    ((SEG, 256, 256), BF),
    ((2, NZ, 8, 256), BF),
    ((NQ, NZ, 8, 256), BF),
    ((NQ, NZ, 8, 256), BF),
    ((NDP, 8, 128), BF),
    ((NZ, NQ, 8, 128), BF),
    ((NQ, NZ, 8, 128), BF),
    ((56, 256), F32),
    ((2, 256, 1024), BF),
    ((2, 256, 1024), BF),
)
TRAIN_SEMS = (0,) + (SEG,) * 8 + (8,) * 14
LOAD_VMEM = (((2, 256, 1024), F32), ((256, 1024), BF), ((512, 128), jnp.int32))
LOAD_SEMS = (2, 0, 0)


def whole_body(*refs):
    images, texts, section, unit, cosine, sine, books, bank, cats, slots, neg = refs[:11]
    wcol, blocks, left, right, loss = refs[11:16]
    groups, at = [], 16
    for part in (ENCODE_VMEM, TRAIN_VMEM, LOAD_VMEM, ENCODE_SEMS, TRAIN_SEMS, LOAD_SEMS):
        groups.append(refs[at : at + len(part)])
        at += len(part)
    encode_vmem, train_vmem, load_vmem, encode_sems, train_sems, load_sems = groups
    pool, wv = encode_vmem[:2]
    books_v, bank_v, neg_v = load_vmem
    book_copies = [
        pltpu.make_async_copy(books.at[level], books_v.at[level], load_sems[0].at[level])
        for level in range(2)
    ]
    bank_copy = pltpu.make_async_copy(bank, bank_v, load_sems[1])
    neg_copy = pltpu.make_async_copy(neg, neg_v, load_sems[2])
    w_copies = encode_body(
        images, texts, section, unit, cosine, sine, pool, wcol, wv, *encode_vmem[2:], *encode_sems,
        [*book_copies, bank_copy, neg_copy],
    )
    train_body(
        pool, w_copies, books_v, bank_v, cats, slots, neg_v, book_copies, bank_copy, neg_copy,
        blocks, left, right, loss, wv, *train_vmem, *train_sems,
    )


def whole(images, texts, section, unit, books, bank, cats, slots, neg):
    half = HEAD_TXT // 2
    exponents = np.arange(half, dtype=np.float32) * np.float32(2.0 / HEAD_TXT)
    inverse = np.exp(np.float32(-math.log(rope_theta)) * exponents).astype(np.float32)
    angles = np.arange(64, dtype=np.float32)[:, None] * inverse[None, :]
    cosine = np.tile(np.cos(angles), (4, 2)).astype(np.float32)
    sine = np.tile(np.concatenate([-np.sin(angles), np.sin(angles)], axis=1), (4, 1))
    anywhere = pl.BlockSpec(memory_space=pl.ANY)
    vmem = pl.BlockSpec(memory_space=pltpu.VMEM)
    dma = pltpu.SemaphoreType.DMA
    buffers = ENCODE_VMEM + TRAIN_VMEM + LOAD_VMEM
    semaphores = ENCODE_SEMS + TRAIN_SEMS + LOAD_SEMS
    return pl.pallas_call(
        whole_body,
        out_shape=(
            jax.ShapeDtypeStruct((NZ, NQ * 56, 256), BF),
            jax.ShapeDtypeStruct((SEG, 56, 256), BF),
            jax.ShapeDtypeStruct((2, 48, 256), BF),
            jax.ShapeDtypeStruct((2, 48, 1024), BF),
            jax.ShapeDtypeStruct((8, 128), F32),
        ),
        in_specs=[anywhere] * 3 + [vmem] * 3 + [anywhere] * 2 + [vmem] * 2 + [anywhere],
        out_specs=(anywhere, vmem, vmem, vmem, vmem),
        scratch_shapes=[pltpu.VMEM(*buffer) for buffer in buffers]
        + [dma((count,)) if count else dma for count in semaphores],
        compiler_params=pltpu.CompilerParams(
            collective_id=0, has_side_effects=True, vmem_limit_bytes=60 << 20
        ),
        name="whole",
    )(
        images,
        texts.reshape(512, 1536),
        section.reshape(21504, 128),
        unit,
        jnp.asarray(cosine, F32),
        jnp.asarray(sine, F32),
        books,
        bank,
        cats,
        slots,
        neg,
    )


def per_device(
    images, texts, section_weights, uniting_weights, codebooks, neg_bank, item_cats, cat_slot, neg_index
):
    books = codebooks.reshape(2, 256, 1024)
    _, blocks, left, right, loss = whole(
        images,
        texts,
        section_weights,
        uniting_weights,
        books,
        neg_bank.reshape(256, 1024),
        item_cats.reshape(SEG, 128),
        cat_slot.reshape(1, NDP),
        neg_index.reshape(512, 128),
    )
    ugrad, bgrad, loss = finish(left, right, books, blocks, loss)
    return ugrad, bgrad.reshape(codebooks.shape), loss


def solution(mesh):
    placed = (
        P("dp", None, None),
        P("dp", None, None),
        P("segment", None, None),
        P("dp", None),
        P("dp", None, None, None),
        P("dp", None, None),
        P(),
        P(),
        P(),
    )
    return jax.shard_map(
        per_device,
        mesh=mesh,
        in_specs=placed,
        out_specs=(P("dp", None), P("dp", None, None, None), P("dp")),
        check_vma=False,
    )
```
